32 devices in a mesh: dp: 16 (over z, x, core), tensor: 2 (over y).
Axes of the slice: x: 2, y: 2, z: 4, core: 2. Of those that a mesh axis runs over, the one named last changes fastest.
Arguments:
- layer_input: bfloat16 [16384, 1536], P(('dp', 'tensor')), may hold values from -6 to 6
- gain_attn: float32 [1536], replicated, may hold values from 0.25 to 1.75
- w_attn: bfloat16 [1536, 4, 1536], P('dp', None, 'tensor'), may hold values from -0.15625 to 0.15625
- w_forget: bfloat16 [1536, 24], P('dp', 'tensor'), may hold values from -0.15625 to 0.15625
- forget_bias: float32 [24], replicated, may hold values from 1.5 to 8
- w_out: bfloat16 [1536, 1536], P('tensor', 'dp'), may hold values from -2.5 to 2.5
- gain_mlp: float32 [1536], replicated, may hold values from 0.25 to 1.75
- w_mlp: bfloat16 [1536, 2, 4096], P('dp', None, 'tensor'), may hold values from -0.15625 to 0.15625
- w_down: bfloat16 [4096, 1536], P('tensor', 'dp'), may hold values from -0.09375 to 0.09375
- lengths: int32 [16], P('dp'), may hold values from 256 to 1024, as said below
- cotangent: bfloat16 [16384, 1536], P(('dp', 'tensor')), may hold values from -6 to 6
Outputs:
- layer_output: bfloat16 [16384, 1536], P(('dp', 'tensor'))
- grad_input: float32 [16384, 1536], P(('dp', 'tensor'))
- grad_gain_attn: float32 [1536], replicated
- grad_w_attn: float32 [1536, 4, 1536], P('dp', None, 'tensor')
- grad_w_forget: float32 [1536, 24], P('dp', 'tensor')
- grad_forget_bias: float32 [24], replicated
- grad_w_out: float32 [1536, 1536], P('tensor', 'dp')
- grad_gain_mlp: float32 [1536], replicated
- grad_w_mlp: float32 [1536, 2, 4096], P('dp', None, 'tensor')
- grad_w_down: float32 [4096, 1536], P('tensor', 'dp')
The draws below stay inside these ranges and needn't reach their ends.
Inputs may be any that keep to these rules, and one draw needn't show every extreme that they name: `lengths`: used slots of each sequence, from its first slot on; some sequence uses all 1024 slots and some only 256.
All inputs are finite; a program needn't handle non-finite values.
Results may differ from the reference program's by a relative error of at most 0.015.
Values may be sent and summed in bfloat16 or wider, within the bound.
No kernel may reach another device: no remote copies, remote signals or barrier semaphores. Data moves between devices by JAX's collectives and lax.ppermute only.
A program may use at most 256 MiB of HBM per device.

```python
import jax
import jax.numpy as jnp
from jax import lax

D = 1536
HEADS = 24
HEAD = 64
FF = 4096
SLOTS = 1024
SEQS = 16
TOKENS = 16384
SHORTEST = 256


def draw_lengths(key, part):
    keys = jax.random.split(key, 3)
    drawn = jax.random.randint(keys[0], (SEQS,), SHORTEST, SLOTS + 1)
    first = jax.random.randint(keys[1], (), 0, SEQS)
    offset = jax.random.randint(keys[2], (), 1, SEQS)
    second = (first + offset) % SEQS
    places = jnp.arange(SEQS)
    drawn = jnp.where(places == first, SLOTS, drawn)
    drawn = jnp.where(places == second, SHORTEST, drawn)
    return drawn.astype(jnp.int32)


def block_levels(stream_key, extent, cuts, low, high):
    def one(position, shards_of):
        heights = jax.random.uniform(jax.random.fold_in(jax.random.fold_in(stream_key, 6), position), (shards_of,), jnp.float32, low / len(cuts), high / len(cuts))
        return jnp.repeat(jnp.exp(heights), extent[position] // shards_of).reshape((-1,) + (1,) * (len(extent) - position - 1))

    factor_of = one(*cuts[0])
    for cut in cuts[1:]:
        factor_of = factor_of * one(*cut)
    return factor_of


def normal_values(key, dims, scale, most, shards=(), held_as=jnp.bfloat16):
    level = block_levels(key, dims, shards, -0.22, 0.18) if shards else 1.0
    values = jax.random.normal(key, dims, jnp.float32) * scale * level
    return jnp.minimum(jnp.maximum(values, -most), most).astype(held_as)


def setup_inputs(seed: int = 0) -> dict:
    key_of = jax.random.split(jax.random.key(seed), 12)
    layer_input = normal_values(key_of[0], (TOKENS, D), 1.0, 6.0, ((0, 32),))
    gain_attn = jnp.clip(1.0 + 0.15 * jax.random.normal(key_of[1], (D,), jnp.float32), 0.25, 1.75)
    w_attn = normal_values(key_of[2], (D, 4, D), D ** -0.5, 0.15625, ((0, 16), (2, 2)))
    w_forget = normal_values(key_of[3], (D, HEADS), D ** -0.5, 0.15625, ((0, 16), (1, 2)))
    forget_bias = jnp.clip(jax.random.uniform(key_of[4], (HEADS,), jnp.float32, 1.5, 8.0), 1.5, 8.0)
    w_out = normal_values(key_of[5], (D, D), (max(D // 256, 1)) ** -0.5, 2.5, ((0, 2), (1, 16)))
    gain_mlp = jnp.clip(1.0 + 0.15 * jax.random.normal(key_of[6], (D,), jnp.float32), 0.25, 1.75)
    w_mlp = normal_values(key_of[7], (D, 2, FF), D ** -0.5, 0.15625, ((0, 16), (2, 2)))
    w_down = normal_values(key_of[8], (FF, D), FF ** -0.5, 0.09375, ((0, 2), (1, 16)))
    lengths = draw_lengths(jax.random.fold_in(key_of[11], 71), 0)
    cotangent = normal_values(key_of[10], (TOKENS, D), 1.0, 6.0, ((0, 32),))
    return dict(layer_input=layer_input, gain_attn=gain_attn, w_attn=w_attn, w_forget=w_forget, forget_bias=forget_bias, w_out=w_out, gain_mlp=gain_mlp, w_mlp=w_mlp, w_down=w_down, lengths=lengths, cotangent=cotangent)


@jax.custom_vjp
def low(v):
    return lax.optimization_barrier(v.astype(jnp.bfloat16)).astype(jnp.float32)

@jax.custom_vjp
def low_back(v):
    return v

def low_keep(v):
    return (low(v), None)

def low_pass(kept, grad):
    return (grad,)

def back_keep(v):
    return (v, None)

def back_low(kept, grad):
    return (low(grad),)
low.defvjp(low_keep, low_pass)
low_back.defvjp(back_keep, back_low)

def rms_scaled(values):
    return values * lax.rsqrt(lax.optimization_barrier(jnp.mean(values * values, axis=-1, keepdims=True)) + 1e-06)

def sequence_attention(packed):
    queries, key_rows, value_rows, log_forget, length = packed
    decays = jnp.cumsum(log_forget, axis=0).T
    scores = jnp.einsum('qhe,khe->hqk', queries, key_rows, precision=lax.Precision.HIGHEST) * HEAD ** (-0.5)
    scores = scores + decays[:, :, None] - decays[:, None, :]
    scores = low_back(scores)
    positions = jnp.arange(SLOTS, dtype=jnp.int32)
    allowed = (positions[None, :] <= positions[:, None]) & (positions[None, :] < length)
    scores = jnp.where(allowed[None], scores, -1e+30)
    soft_low = low(jax.nn.softmax(scores, axis=-1))
    return jnp.einsum('hqk,khe->qhe', soft_low, value_rows, precision=lax.Precision.HIGHEST)

def layer(layer_input, gain_attn, w_attn, w_forget, forget_bias, w_out, gain_mlp, w_mlp, w_down, valid, lengths):
    normed = low(rms_scaled(layer_input) * gain_attn)
    projected = jnp.einsum('td,dkc->tkc', normed, w_attn, precision=lax.Precision.HIGHEST)
    queries = low_back(low(projected[:, 0]))
    key_rows = low_back(low(projected[:, 1]))
    value_rows = low_back(low(projected[:, 2]))
    out_gate = low_back(projected[:, 3])
    forget_logit = low_back(jnp.dot(normed, w_forget, precision=lax.Precision.HIGHEST)) + forget_bias
    log_forget = jax.nn.log_sigmoid(forget_logit)

    def split_heads(values):
        return values.reshape(SEQS, SLOTS, HEADS, HEAD)
    attended = lax.map(jax.checkpoint(sequence_attention), (split_heads(queries), split_heads(key_rows), split_heads(value_rows), log_forget.reshape(SEQS, SLOTS, HEADS), lengths))
    attended = low_back(attended.reshape(TOKENS, D))
    gated = low(attended * jax.nn.sigmoid(out_gate))
    branch = low_back(jnp.dot(gated, w_out, precision=lax.Precision.HIGHEST))
    middle = layer_input + branch
    normed_mlp = low(rms_scaled(middle) * gain_mlp)
    paired = jnp.einsum('td,dkf->tkf', normed_mlp, w_mlp, precision=lax.Precision.HIGHEST)
    gate_pre = low_back(paired[:, 0])
    up_pre = low_back(paired[:, 1])
    hidden = low(jax.nn.silu(gate_pre) * up_pre)
    branch_mlp = low_back(jnp.dot(hidden, w_down, precision=lax.Precision.HIGHEST))
    return valid * (middle + branch_mlp)

def reference(layer_input, gain_attn, w_attn, w_forget, forget_bias, w_out, gain_mlp, w_mlp, w_down, lengths, cotangent):
    positions = jnp.arange(TOKENS, dtype=jnp.int32)
    seq_lengths = lengths[positions // SLOTS]
    valid = (positions % SLOTS < seq_lengths).astype(jnp.float32)[:, None]
    floats = (layer_input.astype(jnp.float32), gain_attn.astype(jnp.float32), w_attn.astype(jnp.float32), w_forget.astype(jnp.float32), forget_bias.astype(jnp.float32), w_out.astype(jnp.float32), gain_mlp.astype(jnp.float32), w_mlp.astype(jnp.float32), w_down.astype(jnp.float32))

    def forward(*params):
        return layer(*params, valid, lengths)
    result, pull = jax.vjp(forward, *floats)
    grads = pull(cotangent.astype(jnp.float32))
    return (result.astype(jnp.bfloat16), grads[0], grads[1], grads[2], grads[3], grads[4], grads[5], grads[6], grads[7], grads[8])
```

```python
import jax
import jax.numpy as jnp
from jax import lax
from jax.sharding import PartitionSpec as P

HEAD = 64
SLOTS = 1024
EPS = 1e-06
PAD = 128

BF16 = jnp.bfloat16
F32 = jnp.float32


def norm_parts(rows):
    inverse = lax.rsqrt(jnp.mean(rows * rows, axis=-1, keepdims=True) + EPS)
    return (rows * inverse, inverse)


def norm_back(grad_normed, scaled, inverse, gain):
    grad_scaled = grad_normed * gain
    inner_sum = jnp.mean(grad_scaled * scaled, axis=-1, keepdims=True)
    return inverse * (grad_scaled - scaled * inner_sum)


def dot_nn(a, b):
    return lax.dot_general(a, b, (((1,), (0,)), ((), ())), preferred_element_type=F32)


def dot_nt(a, b):
    return lax.dot_general(a, b, (((1,), (1,)), ((), ())), preferred_element_type=F32)


def dot_tn(a, b):
    return lax.dot_general(a, b, (((0,), (0,)), ((), ())), preferred_element_type=F32)


def swap(rows):
    return lax.ppermute(rows, "tensor", [(0, 1), (1, 0)])


def share_rows(own):
    if lax.axis_size("tensor") != 2:
        return lax.all_gather(own, "tensor", axis=0, tiled=True)
    other = swap(own)
    first = lax.axis_index("tensor") == 0
    return jnp.concatenate([jnp.where(first, own, other), jnp.where(first, other, own)], axis=0)


def sum_rows(term_fn, own_rows):
    size = lax.axis_size("tensor")
    if size != 2:
        term = term_fn(jnp.int32(0), own_rows * size).astype(BF16)
        return lax.psum_scatter(term, "tensor", scatter_dimension=0, tiled=True).astype(F32)
    index = lax.axis_index("tensor")
    sent = swap(term_fn((1 - index) * own_rows, own_rows).astype(BF16))
    return term_fn(index * own_rows, own_rows) + sent.astype(F32)


def gather_dp(shard):
    return lax.all_gather(shard, "dp", axis=0, tiled=True)


def scatter_dp(grad):
    return lax.psum_scatter(grad, "dp", scatter_dimension=0, tiled=True)


def block_scores(queries, key_rows, decays, length, block_start, block_rows):
    picked = lax.slice_in_dim(queries, block_start, block_start + block_rows, axis=0)
    scores = jnp.einsum(
        "qhe,khe->hqk", picked, key_rows, preferred_element_type=jnp.float32
    ) * HEAD ** (-0.5)
    scores = (
        scores + decays[block_start : block_start + block_rows].T[:, :, None] - decays.T[:, None, :]
    )
    query_pos = block_start + jnp.arange(block_rows, dtype=jnp.int32)
    key_pos = jnp.arange(SLOTS, dtype=jnp.int32)
    allowed = (key_pos[None, :] <= query_pos[:, None]) & (key_pos[None, :] < length)
    return (picked, jnp.where(allowed[None], scores, -1e30), allowed[None])


def sequence_forward(packed):
    queries, key_rows, value_rows, decays, length = packed
    block_rows = min(512, SLOTS)
    outputs = []
    log_totals = []
    for block_start in range(0, SLOTS, block_rows):
        picked, scores, allowed = block_scores(
            queries, key_rows, decays, length, block_start, block_rows
        )
        row_max = jnp.max(scores, axis=-1, keepdims=True)
        exponent = jnp.exp(scores - row_max)
        totals = jnp.sum(exponent, axis=-1, keepdims=True)
        soft_low = (exponent / totals).astype(jnp.bfloat16)
        outputs.append(
            jnp.einsum("hqk,khe->qhe", soft_low, value_rows, preferred_element_type=jnp.float32)
        )
        log_totals.append((row_max + jnp.log(totals))[:, :, 0])
    return (jnp.concatenate(outputs, axis=0), jnp.concatenate(log_totals, axis=1))


def sequence_backward(packed):
    queries, key_rows, value_rows, decays, length, log_totals, grad_attended = packed
    block_rows = min(512, SLOTS)
    score_scale = HEAD ** (-0.5)
    grad_keys = jnp.zeros(key_rows.shape, jnp.float32)
    grad_values = jnp.zeros(value_rows.shape, jnp.float32)
    column_terms = jnp.zeros((decays.shape[1], decays.shape[0]), jnp.float32)
    query_grads = []
    row_terms = []
    for block_start in range(0, SLOTS, block_rows):
        picked, scores, allowed = block_scores(
            queries, key_rows, decays, length, block_start, block_rows
        )
        shifted = scores - log_totals[:, block_start : block_start + block_rows, None]
        soft = jnp.where(allowed, jnp.exp(shifted), 0.0)
        grad_picked = lax.slice_in_dim(grad_attended, block_start, block_start + block_rows, axis=0)
        grad_soft = jnp.einsum(
            "qhe,khe->hqk", grad_picked, value_rows, preferred_element_type=jnp.float32
        )
        inner_sum = jnp.sum(soft * grad_soft, axis=-1, keepdims=True)
        grad_scores = (soft * (grad_soft - inner_sum)).astype(jnp.bfloat16)
        query_grads.append(
            jnp.einsum("hqk,khe->qhe", grad_scores, key_rows, preferred_element_type=jnp.float32)
            * score_scale
        )
        grad_keys = (
            grad_keys
            + jnp.einsum("hqk,qhe->khe", grad_scores, picked, preferred_element_type=jnp.float32)
            * score_scale
        )
        grad_values = grad_values + jnp.einsum(
            "hqk,qhe->khe",
            soft.astype(jnp.bfloat16),
            grad_picked,
            preferred_element_type=jnp.float32,
        )
        wide_grads = grad_scores.astype(jnp.float32)
        row_terms.append(jnp.sum(wide_grads, axis=2))
        column_terms = column_terms - jnp.sum(wide_grads, axis=1)
    grad_decay = jnp.concatenate(row_terms, axis=1) + column_terms
    grad_forget = jnp.cumsum(grad_decay[:, ::-1], axis=1)[:, ::-1].T
    return (
        jnp.concatenate(query_grads, axis=0).astype(jnp.bfloat16),
        grad_keys.astype(jnp.bfloat16),
        grad_values.astype(jnp.bfloat16),
        grad_forget,
    )


def on_device(
    layer_input,
    gain_attn,
    w_attn,
    w_forget,
    forget_bias,
    w_out,
    gain_mlp,
    w_mlp,
    w_down,
    lengths,
    cotangent,
):
    own_rows, width = layer_input.shape
    group_seqs = lengths.shape[0]
    group_rows = group_seqs * SLOTS
    part = w_attn.shape[2]
    heads_dev = part // HEAD
    units = w_mlp.shape[2]
    own_d = w_attn.shape[0]
    tensor_index = lax.axis_index("tensor")
    bias_own = lax.dynamic_slice_in_dim(forget_bias, tensor_index * heads_dev, heads_dev)
    positions = tensor_index * own_rows + jnp.arange(own_rows, dtype=jnp.int32)
    seq_of_row = positions // SLOTS
    matches = seq_of_row[:, None] == jnp.arange(group_seqs, dtype=jnp.int32)[None, :]
    own_lengths = jnp.sum(jnp.where(matches, lengths[None, :], 0), axis=1)
    valid = (positions % SLOTS < own_lengths).astype(F32)[:, None]

    attn_shard = jnp.concatenate(
        [w_attn.reshape(own_d, 4 * part), jnp.pad(w_forget, ((0, 0), (0, PAD - heads_dev)))], axis=1
    )
    attn_full = gather_dp(attn_shard)
    out_full = gather_dp(w_out.T)
    down_full = gather_dp(w_down.T)
    mlp_full = gather_dp(w_mlp.reshape(own_d, 2 * units))

    input_wide = layer_input.astype(F32)
    scaled_attn, inverse_attn = norm_parts(input_wide)
    normed_all = share_rows((scaled_attn * gain_attn).astype(BF16))
    grad_final = cotangent.astype(F32) * valid
    grad_final_all = share_rows(grad_final.astype(BF16))

    proj = dot_nn(normed_all, attn_full[:, : 3 * part]).astype(BF16)
    gate_logit = dot_nn(normed_all, attn_full[:, 3 * part :])
    out_gate = gate_logit[:, :part]
    logits = gate_logit[:, part : part + heads_dev] + bias_own

    def split_heads(column):
        return proj[:, column * part : (column + 1) * part].reshape(
            group_seqs, SLOTS, heads_dev, HEAD
        )

    queries, key_rows, value_rows = (split_heads(0), split_heads(1), split_heads(2))
    log_forget = jax.nn.log_sigmoid(logits)
    decays = jnp.cumsum(log_forget.reshape(group_seqs, SLOTS, heads_dev), axis=1)
    attended, log_totals = lax.map(
        sequence_forward, (queries, key_rows, value_rows, decays, lengths)
    )
    attended = attended.reshape(group_rows, part)
    gate_sig = jax.nn.sigmoid(out_gate)
    gated = (attended * gate_sig).astype(BF16)

    def attn_term(first_row, row_count):
        return dot_nt(lax.dynamic_slice_in_dim(gated, first_row, row_count), out_full)

    middle = input_wide + sum_rows(attn_term, own_rows)
    scaled_mlp, inverse_mlp = norm_parts(middle)
    normed_mid = share_rows((scaled_mlp * gain_mlp).astype(BF16))
    grad_hidden = dot_nn(grad_final_all, down_full)
    gate_pre = dot_nn(normed_mid, mlp_full[:, :units])
    up_pre = dot_nn(normed_mid, mlp_full[:, units:])
    gate_s = jax.nn.sigmoid(gate_pre)
    silu = gate_pre * gate_s
    hidden = (silu * up_pre).astype(BF16)
    grad_gate = (grad_hidden * up_pre * gate_s * (1.0 + gate_pre * (1.0 - gate_s))).astype(BF16)
    grad_up = (grad_hidden * silu).astype(BF16)
    grad_pair = jnp.concatenate([grad_gate, grad_up], axis=1)

    def mlp_back_term(first_row, row_count):
        return dot_nt(lax.dynamic_slice_in_dim(grad_pair, first_row, row_count), mlp_full)

    grad_normed_mlp = sum_rows(mlp_back_term, own_rows)
    down_part = scatter_dp(dot_tn(grad_final_all, hidden).astype(BF16))
    mlp_part = scatter_dp(dot_tn(normed_mid, grad_pair).astype(BF16))

    gain_mlp_part = jnp.sum(scaled_mlp * grad_normed_mlp, axis=0)
    grad_middle = grad_final + norm_back(grad_normed_mlp, scaled_mlp, inverse_mlp, gain_mlp)
    grad_branch_all = share_rows(grad_middle.astype(BF16))

    def mlp_term(first_row, row_count):
        return dot_nt(lax.dynamic_slice_in_dim(hidden, first_row, row_count), down_full)

    layer_output = (valid * (middle + sum_rows(mlp_term, own_rows))).astype(BF16)

    grad_gated = dot_nn(grad_branch_all, out_full)
    out_part = scatter_dp(dot_tn(grad_branch_all, gated).astype(BF16))
    grad_attended = (grad_gated * gate_sig).astype(BF16)
    grad_out_gate = (grad_gated * attended * gate_sig * (1.0 - gate_sig)).astype(BF16)
    grad_heads = grad_attended.reshape(group_seqs, SLOTS, heads_dev, HEAD)
    grad_queries, grad_keys, grad_values, grad_forget = lax.map(
        sequence_backward, (queries, key_rows, value_rows, decays, lengths, log_totals, grad_heads)
    )
    grad_logit = grad_forget.reshape(group_rows, heads_dev) * jax.nn.sigmoid(-logits)
    bias_part = jnp.sum(grad_logit, axis=0)
    grad_proj = jnp.concatenate(
        [
            grad_queries.reshape(group_rows, part),
            grad_keys.reshape(group_rows, part),
            grad_values.reshape(group_rows, part),
            grad_out_gate,
            jnp.pad(grad_logit.astype(BF16), ((0, 0), (0, PAD - heads_dev))),
        ],
        axis=1,
    )
    attn_part = scatter_dp(dot_tn(normed_all, grad_proj).astype(BF16))

    def attn_back_term(first_row, row_count):
        return dot_nt(lax.dynamic_slice_in_dim(grad_proj, first_row, row_count), attn_full)

    grad_normed_attn = sum_rows(attn_back_term, own_rows)
    gain_attn_part = jnp.sum(scaled_attn * grad_normed_attn, axis=0)
    grad_input = grad_middle + norm_back(grad_normed_attn, scaled_attn, inverse_attn, gain_attn)
    bias_full = lax.dynamic_update_slice_in_dim(
        jnp.zeros(forget_bias.shape, F32), bias_part, tensor_index * heads_dev, 0
    )
    grad_gain_attn, grad_gain_mlp, grad_forget_bias = lax.psum(
        (gain_attn_part, gain_mlp_part, bias_full), ("dp", "tensor")
    )
    attn_part = attn_part.astype(F32)
    return (
        layer_output,
        grad_input,
        grad_gain_attn,
        attn_part[:, : 4 * part].reshape(own_d, 4, part),
        attn_part[:, 4 * part : 4 * part + heads_dev],
        grad_forget_bias,
        out_part.astype(F32).T,
        grad_gain_mlp,
        mlp_part.astype(F32).reshape(own_d, 2, units),
        down_part.astype(F32).T,
    )


def solution(mesh):
    placed = (
        P(("dp", "tensor"), None),
        P(),
        P("dp", None, "tensor"),
        P("dp", "tensor"),
        P(),
        P("tensor", "dp"),
        P(),
        P("dp", None, "tensor"),
        P("tensor", "dp"),
        P("dp"),
        P(("dp", "tensor"), None),
    )
    return jax.shard_map(
        on_device,
        mesh=mesh,
        in_specs=placed,
        out_specs=(
            P(("dp", "tensor"), None),
            P(("dp", "tensor"), None),
            P(),
            P("dp", None, "tensor"),
            P("dp", "tensor"),
            P(),
            P("tensor", "dp"),
            P(),
            P("dp", None, "tensor"),
            P("tensor", "dp"),
        ),
        check_vma=False,
    )
```

```python
import functools

import jax
import jax.numpy as jnp
from jax import lax
from jax.experimental import pallas as pl
from jax.experimental.pallas import tpu as pltpu
from jax.sharding import PartitionSpec as P

HEAD = 64
SLOTS = 1024
EPS = 1e-06
PAD = 128
BLOCK = 256
NEG = -1e30

BF16 = jnp.bfloat16
F32 = jnp.float32


def norm_parts(rows):
    inverse = lax.rsqrt(jnp.mean(rows * rows, axis=-1, keepdims=True) + EPS)
    return (rows * inverse, inverse)


def norm_back(grad_normed, scaled, inverse, gain):
    grad_scaled = grad_normed * gain
    inner_sum = jnp.mean(grad_scaled * scaled, axis=-1, keepdims=True)
    return inverse * (grad_scaled - scaled * inner_sum)


def dot_nn(a, b):
    return lax.dot_general(a, b, (((1,), (0,)), ((), ())), preferred_element_type=F32)


def dot_nt(a, b):
    return lax.dot_general(a, b, (((1,), (1,)), ((), ())), preferred_element_type=F32)


def dot_tn(a, b):
    return lax.dot_general(a, b, (((0,), (0,)), ((), ())), preferred_element_type=F32)


def swap(rows):
    return lax.ppermute(rows, "tensor", [(0, 1), (1, 0)])


def share_rows(own):
    if lax.axis_size("tensor") != 2:
        return lax.all_gather(own, "tensor", axis=0, tiled=True)
    other = swap(own)
    first = lax.axis_index("tensor") == 0
    return jnp.concatenate([jnp.where(first, own, other), jnp.where(first, other, own)], axis=0)


def sum_rows(term_fn, own_rows):
    size = lax.axis_size("tensor")
    if size != 2:
        term = term_fn(jnp.int32(0), own_rows * size).astype(BF16)
        return lax.psum_scatter(term, "tensor", scatter_dimension=0, tiled=True).astype(F32)
    index = lax.axis_index("tensor")
    sent = swap(term_fn((1 - index) * own_rows, own_rows).astype(BF16))
    return term_fn(index * own_rows, own_rows) + sent.astype(F32)


def gather_dp(shard):
    return lax.all_gather(shard, "dp", axis=0, tiled=True)


def scatter_dp(grad):
    return lax.psum_scatter(grad, "dp", scatter_dimension=0, tiled=True)


def head_span(lane, head):
    return (lane >= head * HEAD) & (lane < (head + 1) * HEAD)


def key_side(keys, bias, lane, head, spare):
    high = bias.astype(BF16).astype(F32)
    rest = bias - high
    mid = rest.astype(BF16).astype(F32)
    extra = jnp.where(
        lane == spare,
        high,
        jnp.where(lane == spare + 1, mid, jnp.where(lane == spare + 2, rest - mid, 0.0)),
    )
    return jnp.where(head_span(lane, head), keys, extra).astype(BF16)


def query_side(queries, lane, head, spare):
    ones = jnp.where((lane >= spare) & (lane < spare + 3), 1.0, 0.0)
    return jnp.where(head_span(lane, head), queries * HEAD ** (-0.5), ones).astype(BF16)


def pick_lane(rows, lane, index):
    return jnp.sum(jnp.where(lane == index, rows, 0.0), axis=1, keepdims=True)


def running_sum(rows, reverse):
    step = 1
    while step < SLOTS:
        zeros = jnp.zeros((step, rows.shape[1]), F32)
        if reverse:
            moved = jnp.concatenate([rows[step:], zeros], axis=0)
        else:
            moved = jnp.concatenate([zeros, rows[:-step]], axis=0)
        rows = rows + moved
        step *= 2
    return rows


def causal(block):
    key = lax.broadcasted_iota(jnp.int32, (block, block), 0)
    query = lax.broadcasted_iota(jnp.int32, (block, block), 1)
    return key <= query


def attend_body(
    lengths, q_ref, k_ref, v_ref, gate_ref, logit_ref, bias_ref, gated_ref, att_ref, shift_ref, keyb_ref,
    *, per_group,
):
    seq = pl.program_id(0)
    group = pl.program_id(1)
    wide = per_group * HEAD

    @pl.when(group == 0)
    def _():
        logit = logit_ref[...] + bias_ref[0:1]
        forget = jnp.minimum(logit, 0.0) - jnp.log1p(jnp.exp(-jnp.abs(logit)))
        slot = lax.broadcasted_iota(jnp.int32, (SLOTS, PAD), 0)
        keyb_ref[...] = jnp.where(slot < lengths[seq], -running_sum(forget, False), NEG)

    lane = lax.broadcasted_iota(jnp.int32, (SLOTS, wide), 1)
    lane_all = lax.broadcasted_iota(jnp.int32, (SLOTS, PAD), 1)
    queries = q_ref[...].astype(F32)
    keys = k_ref[...].astype(F32)
    values_t = jnp.transpose(v_ref[...].astype(F32)).astype(BF16)
    allowed = causal(BLOCK)
    sides = []
    for head in range(per_group):
        spare = HEAD if head == 0 else 0
        bias = pick_lane(keyb_ref[...], lane_all, group * per_group + head)
        sides.append(
            (key_side(keys, bias, lane, head, spare), query_side(queries, lane, head, spare))
        )
    for start in range(0, SLOTS, BLOCK):
        stop = start + BLOCK
        outs = []
        for head in range(per_group):
            key_aug, query_aug = sides[head]
            picked = query_aug[start:stop]
            diag = jnp.where(allowed, dot_nt(key_aug[start:stop], picked), NEG)
            top = jnp.max(diag, axis=0, keepdims=True)
            if start:
                early = dot_nt(key_aug[:start], picked)
                top = jnp.maximum(top, jnp.max(early, axis=0, keepdims=True))
            diag = jnp.exp(diag - top)
            total = jnp.sum(diag, axis=0, keepdims=True)
            value_rows = values_t[head * HEAD : (head + 1) * HEAD]
            out = dot_nn(value_rows[:, start:stop], diag.astype(BF16))
            if start:
                early = jnp.exp(early - top)
                total = total + jnp.sum(early, axis=0, keepdims=True)
                out = out + dot_nn(value_rows[:, :start], early.astype(BF16))
            outs.append(out / total)
            shift_ref[pl.ds(group * per_group + head, 1), start:stop] = -(top + jnp.log(total))
        block = jnp.transpose(jnp.concatenate(outs, axis=0))
        att_ref[start:stop] = block.astype(BF16)
        gated_ref[start:stop] = (block * jax.nn.sigmoid(gate_ref[start:stop])).astype(BF16)


def attend_back_body(
    q_ref, k_ref, v_ref, gate_ref, att_ref, grad_ref, logit_ref, bias_ref, shift_ref, keyb_ref,
    out_ref, bias_out_ref, low_ref, dk_ref, dv_ref, row_ref, col_ref,
    *, per_group, groups,
):
    group = pl.program_id(1)
    wide = per_group * HEAD
    part = groups * wide

    def columns(which):
        if groups == 1:
            return slice(which * part, which * part + wide)
        return pl.ds(pl.multiple_of(which * part + group * wide, wide), wide)

    @pl.when(group == 0)
    def _():
        row_ref[...] = jnp.zeros(row_ref.shape, F32)
        col_ref[...] = jnp.zeros(col_ref.shape, F32)

    lane = lax.broadcasted_iota(jnp.int32, (SLOTS, wide), 1)
    lane_all = lax.broadcasted_iota(jnp.int32, (SLOTS, PAD), 1)
    sig = jax.nn.sigmoid(gate_ref[...])
    grad_gated = grad_ref[...].astype(F32)
    grad_att = grad_gated * sig
    out_ref[:, columns(3)] = (grad_att * att_ref[...].astype(F32) * (1.0 - sig)).astype(BF16)
    low_ref[...] = grad_att.astype(BF16)
    queries = q_ref[...].astype(F32)
    keys = k_ref[...].astype(F32)
    keys_t = jnp.transpose(keys).astype(BF16)
    ones = jnp.ones((16, SLOTS), BF16)
    allowed = causal(BLOCK)
    grad_low = low_ref[...].astype(F32)
    sides = []
    for head in range(per_group):
        spare = HEAD if head == 0 else 0
        bias = pick_lane(keyb_ref[...], lane_all, group * per_group + head)
        sides.append(
            (
                key_side(keys, bias, lane, head, spare),
                query_side(queries, lane, head, spare),
                jnp.where(head_span(lane, head), grad_low, 0.0).astype(BF16),
                jnp.concatenate([keys_t[head * HEAD : (head + 1) * HEAD], ones], axis=0),
            )
        )
    for start in reversed(range(0, SLOTS, BLOCK)):
        stop = start + BLOCK
        last = stop == SLOTS
        outs = []
        for head in range(per_group):
            key_aug, query_aug, grad_own, key_rows = sides[head]
            picked = query_aug[start:stop]
            grads = grad_own[start:stop]
            shift = shift_ref[pl.ds(group * per_group + head, 1), start:stop]
            spans = [(start, stop)] + ([(0, start)] if start else [])
            weights = []
            inner = jnp.zeros((1, BLOCK), F32)
            for low, high in spans:
                score = dot_nt(key_aug[low:high], picked) + shift
                if low == start:
                    score = jnp.where(allowed, score, NEG)
                soft = jnp.exp(score)
                grad_soft = dot_nt(v_ref[low:high], grads)
                inner = inner + jnp.sum(soft * grad_soft, axis=0, keepdims=True)
                weights.append((soft, grad_soft))
            out = jnp.zeros((HEAD + 16, BLOCK), F32)
            for (low, high), (soft, grad_soft) in zip(spans, weights):
                grad_score = (soft * (grad_soft - inner)).astype(BF16)
                key_part = dot_nn(grad_score, picked)
                value_part = dot_nn(soft.astype(BF16), grads)
                if last:
                    dk_ref[head, low:high] = key_part
                    if head == 0:
                        dv_ref[low:high] = value_part
                    else:
                        dv_ref[low:high] += value_part
                else:
                    dk_ref[head, low:high] += key_part
                    dv_ref[low:high] += value_part
                out = out + dot_nn(key_rows[:, low:high], grad_score)
            outs.append(out[:HEAD] * HEAD ** (-0.5))
            row_ref[pl.ds(group * per_group + head, 1), start:stop] = out[HEAD : HEAD + 1]
        out_ref[start:stop, columns(0)] = jnp.transpose(jnp.concatenate(outs, axis=0)).astype(BF16)
    grad_keys = dk_ref[0]
    for head in range(per_group):
        spare = HEAD if head == 0 else 0
        found = dk_ref[head]
        if head:
            grad_keys = jnp.where(head_span(lane, head), found, grad_keys)
        sums = pick_lane(found, lane, spare)
        col_ref[...] = jnp.where(lane_all == group * per_group + head, sums, col_ref[...])
    out_ref[:, columns(1)] = grad_keys.astype(BF16)
    out_ref[:, columns(2)] = dv_ref[...].astype(BF16)

    @pl.when(group == groups - 1)
    def _():
        grad_decay = jnp.transpose(row_ref[...]) - col_ref[...]
        logit = logit_ref[...] + bias_ref[0:1]
        grad_logit = running_sum(grad_decay, True) * jax.nn.sigmoid(-logit)
        out_ref[:, 4 * part :] = grad_logit.astype(BF16)
        bias_out_ref[...] = jnp.broadcast_to(jnp.sum(grad_logit, axis=0, keepdims=True), (8, PAD))


def head_blocks(part):
    heads = part // HEAD
    per_group = 2 if heads % 2 == 0 else heads
    groups = heads // per_group
    wide = per_group * HEAD

    def of(array, which, count):
        if part % 128 == 0:
            return array, pl.BlockSpec((SLOTS, wide), lambda s, g: (s, which * groups + g))
        return (
            array[:, which * part : (which + 1) * part],
            pl.BlockSpec((SLOTS, wide), lambda s, g: (s, g)),
        )

    return per_group, groups, wide, of


def logit_block(gate_logit, part):
    if part % PAD == 0:
        return gate_logit, pl.BlockSpec((SLOTS, PAD), lambda s, g: (s, part // PAD))
    return gate_logit[:, part:], pl.BlockSpec((SLOTS, PAD), lambda s, g: (s, 0))


def attend(proj, gate_logit, bias_rows, lengths, part):
    rows = proj.shape[0]
    seqs = rows // SLOTS
    per_group, groups, wide, of = head_blocks(part)
    fix = lambda f: (lambda s, g, lengths: f(s, g))
    parts = [of(proj, 0, 3), of(proj, 1, 3), of(proj, 2, 3), of(gate_logit, 0, 1)]
    parts.append(logit_block(gate_logit, part))
    parts.append((bias_rows, pl.BlockSpec((8, PAD), lambda s, g: (0, 0))))
    wide_spec = pl.BlockSpec((SLOTS, wide), lambda s, g: (s, g))
    outs = [
        (jax.ShapeDtypeStruct((rows, part), BF16), wide_spec),
        (jax.ShapeDtypeStruct((rows, part), BF16), wide_spec),
        (jax.ShapeDtypeStruct((seqs * PAD, SLOTS), F32), pl.BlockSpec((PAD, SLOTS), lambda s, g: (s, 0))),
        (jax.ShapeDtypeStruct((rows, PAD), F32), pl.BlockSpec((SLOTS, PAD), lambda s, g: (s, 0))),
    ]
    respec = lambda spec: pl.BlockSpec(spec.block_shape, fix(spec.index_map))
    return pl.pallas_call(
        functools.partial(attend_body, per_group=per_group),
        out_shape=[shape for shape, _ in outs],
        grid_spec=pltpu.PrefetchScalarGridSpec(
            num_scalar_prefetch=1,
            grid=(seqs, groups),
            in_specs=[respec(spec) for _, spec in parts],
            out_specs=[respec(spec) for _, spec in outs],
        ),
        compiler_params=pltpu.CompilerParams(
            dimension_semantics=("arbitrary", "arbitrary"), vmem_limit_bytes=48 * 2**20
        ),
        name="attend",
    )(lengths, *[array for array, _ in parts])


def attend_back(proj, gate_logit, attended, grad_gated, bias_rows, shift, keyb, part):
    rows = proj.shape[0]
    seqs = rows // SLOTS
    per_group, groups, wide, of = head_blocks(part)
    parts = [of(proj, 0, 3), of(proj, 1, 3), of(proj, 2, 3), of(gate_logit, 0, 1)]
    parts += [of(attended, 0, 1), of(grad_gated, 0, 1)]
    parts.append(logit_block(gate_logit, part))
    parts.append((bias_rows, pl.BlockSpec((8, PAD), lambda s, g: (0, 0))))
    parts.append((shift, pl.BlockSpec((PAD, SLOTS), lambda s, g: (s, 0))))
    parts.append((keyb, pl.BlockSpec((SLOTS, PAD), lambda s, g: (s, 0))))
    total = 4 * part + PAD
    return pl.pallas_call(
        functools.partial(attend_back_body, per_group=per_group, groups=groups),
        out_shape=[
            jax.ShapeDtypeStruct((rows, total), BF16),
            jax.ShapeDtypeStruct((seqs * 8, PAD), F32),
        ],
        grid=(seqs, groups),
        in_specs=[spec for _, spec in parts],
        out_specs=[
            pl.BlockSpec((SLOTS, total), lambda s, g: (s, 0)),
            pl.BlockSpec((8, PAD), lambda s, g: (s, 0)),
        ],
        scratch_shapes=[
            pltpu.VMEM((SLOTS, wide), BF16),
            pltpu.VMEM((per_group, SLOTS, wide), F32),
            pltpu.VMEM((SLOTS, wide), F32),
            pltpu.VMEM((PAD, SLOTS), F32),
            pltpu.VMEM((SLOTS, PAD), F32),
        ],
        compiler_params=pltpu.CompilerParams(
            dimension_semantics=("arbitrary", "arbitrary"), vmem_limit_bytes=56 * 2**20
        ),
        name="attend_back",
    )(*[array for array, _ in parts])


def on_device(
    layer_input,
    gain_attn,
    w_attn,
    w_forget,
    forget_bias,
    w_out,
    gain_mlp,
    w_mlp,
    w_down,
    lengths,
    cotangent,
):
    own_rows, width = layer_input.shape
    group_seqs = lengths.shape[0]
    group_rows = group_seqs * SLOTS
    part = w_attn.shape[2]
    heads_dev = part // HEAD
    units = w_mlp.shape[2]
    own_d = w_attn.shape[0]
    tensor_index = lax.axis_index("tensor")
    bias_own = lax.dynamic_slice_in_dim(forget_bias, tensor_index * heads_dev, heads_dev)
    positions = tensor_index * own_rows + jnp.arange(own_rows, dtype=jnp.int32)
    seq_of_row = positions // SLOTS
    matches = seq_of_row[:, None] == jnp.arange(group_seqs, dtype=jnp.int32)[None, :]
    own_lengths = jnp.sum(jnp.where(matches, lengths[None, :], 0), axis=1)
    valid = (positions % SLOTS < own_lengths).astype(F32)[:, None]

    attn_shard = jnp.concatenate(
        [w_attn.reshape(own_d, 4 * part), jnp.pad(w_forget, ((0, 0), (0, PAD - heads_dev)))], axis=1
    )
    attn_full = gather_dp(attn_shard)
    out_full = gather_dp(w_out.T)
    down_full = gather_dp(w_down.T)
    mlp_full = gather_dp(w_mlp.reshape(own_d, 2 * units))

    input_wide = layer_input.astype(F32)
    scaled_attn, inverse_attn = norm_parts(input_wide)
    normed_all = share_rows((scaled_attn * gain_attn).astype(BF16))
    grad_final = cotangent.astype(F32) * valid
    grad_final_all = share_rows(grad_final.astype(BF16))

    proj = dot_nn(normed_all, attn_full[:, : 3 * part]).astype(BF16)
    gate_logit = dot_nn(normed_all, attn_full[:, 3 * part :])
    bias_rows = jnp.broadcast_to(jnp.pad(bias_own, (0, PAD - heads_dev))[None, :], (8, PAD))
    gated, attended, shift, keyb = attend(proj, gate_logit, bias_rows, lengths, part)

    def attn_term(first_row, row_count):
        return dot_nt(lax.dynamic_slice_in_dim(gated, first_row, row_count), out_full)

    middle = input_wide + sum_rows(attn_term, own_rows)
    scaled_mlp, inverse_mlp = norm_parts(middle)
    normed_mid = share_rows((scaled_mlp * gain_mlp).astype(BF16))
    grad_hidden = dot_nn(grad_final_all, down_full)
    gate_pre = dot_nn(normed_mid, mlp_full[:, :units])
    up_pre = dot_nn(normed_mid, mlp_full[:, units:])
    gate_s = jax.nn.sigmoid(gate_pre)
    silu = gate_pre * gate_s
    hidden = (silu * up_pre).astype(BF16)
    grad_gate = (grad_hidden * up_pre * gate_s * (1.0 + gate_pre * (1.0 - gate_s))).astype(BF16)
    grad_up = (grad_hidden * silu).astype(BF16)
    grad_pair = jnp.concatenate([grad_gate, grad_up], axis=1)

    def mlp_back_term(first_row, row_count):
        return dot_nt(lax.dynamic_slice_in_dim(grad_pair, first_row, row_count), mlp_full)

    grad_normed_mlp = sum_rows(mlp_back_term, own_rows)
    down_part = scatter_dp(dot_tn(grad_final_all, hidden).astype(BF16))
    mlp_part = scatter_dp(dot_tn(normed_mid, grad_pair).astype(BF16))

    gain_mlp_part = jnp.sum(scaled_mlp * grad_normed_mlp, axis=0)
    grad_middle = grad_final + norm_back(grad_normed_mlp, scaled_mlp, inverse_mlp, gain_mlp)
    grad_branch_all = share_rows(grad_middle.astype(BF16))

    def mlp_term(first_row, row_count):
        return dot_nt(lax.dynamic_slice_in_dim(hidden, first_row, row_count), down_full)

    layer_output = (valid * (middle + sum_rows(mlp_term, own_rows))).astype(BF16)

    grad_gated = dot_nn(grad_branch_all, out_full).astype(BF16)
    out_part = scatter_dp(dot_tn(grad_branch_all, gated).astype(BF16))
    grad_proj, bias_sums = attend_back(
        proj, gate_logit, attended, grad_gated, bias_rows, shift, keyb, part
    )
    bias_part = jnp.sum(bias_sums.reshape(group_seqs, 8, PAD)[:, 0, :heads_dev], axis=0)
    attn_part = scatter_dp(dot_tn(normed_all, grad_proj).astype(BF16))

    def attn_back_term(first_row, row_count):
        return dot_nt(lax.dynamic_slice_in_dim(grad_proj, first_row, row_count), attn_full)

    grad_normed_attn = sum_rows(attn_back_term, own_rows)
    gain_attn_part = jnp.sum(scaled_attn * grad_normed_attn, axis=0)
    grad_input = grad_middle + norm_back(grad_normed_attn, scaled_attn, inverse_attn, gain_attn)
    bias_full = lax.dynamic_update_slice_in_dim(
        jnp.zeros(forget_bias.shape, F32), bias_part, tensor_index * heads_dev, 0
    )
    grad_gain_attn, grad_gain_mlp, grad_forget_bias = lax.psum(
        (gain_attn_part, gain_mlp_part, bias_full), ("dp", "tensor")
    )
    attn_part = attn_part.astype(F32)
    return (
        layer_output,
        grad_input,
        grad_gain_attn,
        attn_part[:, : 4 * part].reshape(own_d, 4, part),
        attn_part[:, 4 * part : 4 * part + heads_dev],
        grad_forget_bias,
        out_part.astype(F32).T,
        grad_gain_mlp,
        mlp_part.astype(F32).reshape(own_d, 2, units),
        down_part.astype(F32).T,
    )


def solution(mesh):
    placed = (
        P(("dp", "tensor"), None),
        P(),
        P("dp", None, "tensor"),
        P("dp", "tensor"),
        P(),
        P("tensor", "dp"),
        P(),
        P("dp", None, "tensor"),
        P("tensor", "dp"),
        P("dp"),
        P(("dp", "tensor"), None),
    )
    return jax.shard_map(
        on_device,
        mesh=mesh,
        in_specs=placed,
        out_specs=(
            P(("dp", "tensor"), None),
            P(("dp", "tensor"), None),
            P(),
            P("dp", None, "tensor"),
            P("dp", "tensor"),
            P(),
            P("tensor", "dp"),
            P(),
            P("dp", None, "tensor"),
            P("tensor", "dp"),
        ),
        check_vma=False,
    )
```

```python
import functools

import jax
import jax.numpy as jnp
from jax import lax
from jax.experimental import pallas as pl
from jax.experimental.pallas import tpu as pltpu
from jax.sharding import PartitionSpec as P

HEAD = 64
SLOTS = 1024
EPS = 1e-06
PAD = 128
BLOCK = 256
NEG = -1e30

BF16 = jnp.bfloat16
F32 = jnp.float32


def norm_parts(rows):
    inverse = lax.rsqrt(jnp.mean(rows * rows, axis=-1, keepdims=True) + EPS)
    return (rows * inverse, inverse)


def norm_back(grad_normed, scaled, inverse, gain):
    grad_scaled = grad_normed * gain
    inner_sum = jnp.mean(grad_scaled * scaled, axis=-1, keepdims=True)
    return inverse * (grad_scaled - scaled * inner_sum)


def dot_nn(a, b):
    return lax.dot_general(a, b, (((1,), (0,)), ((), ())), preferred_element_type=F32)


def dot_nt(a, b):
    return lax.dot_general(a, b, (((1,), (1,)), ((), ())), preferred_element_type=F32)


def dot_tn(a, b):
    return lax.dot_general(a, b, (((0,), (0,)), ((), ())), preferred_element_type=F32)


def swap(rows):
    return lax.ppermute(rows, "tensor", [(0, 1), (1, 0)])


def share_rows(own):
    if lax.axis_size("tensor") != 2:
        return lax.all_gather(own, "tensor", axis=0, tiled=True)
    other = swap(own)
    first = lax.axis_index("tensor") == 0
    return jnp.concatenate([jnp.where(first, own, other), jnp.where(first, other, own)], axis=0)


def hold(*values):
    return lax.optimization_barrier(values)


def term_parts(term_fn, own_rows):
    size = lax.axis_size("tensor")
    if size != 2:
        return (term_fn(jnp.int32(0), own_rows * size).astype(BF16), jnp.zeros((), F32))
    index = lax.axis_index("tensor")
    return (
        term_fn((1 - index) * own_rows, own_rows).astype(BF16),
        term_fn(index * own_rows, own_rows),
    )


def cross(leaving):
    if lax.axis_size("tensor") != 2:
        return lax.psum_scatter(leaving, "tensor", scatter_dimension=0, tiled=True)
    return swap(leaving)


def gather_dp(shard):
    return lax.all_gather(shard, "dp", axis=0, tiled=True)


def scatter_dp(grad):
    return lax.psum_scatter(grad, "dp", scatter_dimension=0, tiled=True)


def head_span(lane, head):
    return (lane >= head * HEAD) & (lane < (head + 1) * HEAD)


def key_side(keys, bias, lane, head, spare):
    high = bias.astype(BF16).astype(F32)
    rest = bias - high
    mid = rest.astype(BF16).astype(F32)
    extra = jnp.where(
        lane == spare,
        high,
        jnp.where(lane == spare + 1, mid, jnp.where(lane == spare + 2, rest - mid, 0.0)),
    )
    return jnp.where(head_span(lane, head), keys, extra).astype(BF16)


def query_side(queries, lane, head, spare):
    ones = jnp.where((lane >= spare) & (lane < spare + 3), 1.0, 0.0)
    return jnp.where(head_span(lane, head), queries * HEAD ** (-0.5), ones).astype(BF16)


def pick_lane(rows, lane, index):
    return jnp.sum(jnp.where(lane == index, rows, 0.0), axis=1, keepdims=True)


def running_sum(rows, reverse):
    step = 1
    while step < SLOTS:
        zeros = jnp.zeros((step, rows.shape[1]), F32)
        if reverse:
            moved = jnp.concatenate([rows[step:], zeros], axis=0)
        else:
            moved = jnp.concatenate([zeros, rows[:-step]], axis=0)
        rows = rows + moved
        step *= 2
    return rows


def causal(block):
    key = lax.broadcasted_iota(jnp.int32, (block, block), 0)
    query = lax.broadcasted_iota(jnp.int32, (block, block), 1)
    return key <= query


def attend_body(
    lengths, q_ref, k_ref, v_ref, gate_ref, logit_ref, bias_ref, gated_ref, att_ref, shift_ref, keyb_ref,
    *, per_group,
):
    seq = pl.program_id(0)
    group = pl.program_id(1)
    wide = per_group * HEAD

    @pl.when(group == 0)
    def _():
        logit = logit_ref[...] + bias_ref[0:1]
        forget = jnp.minimum(logit, 0.0) - jnp.log1p(jnp.exp(-jnp.abs(logit)))
        slot = lax.broadcasted_iota(jnp.int32, (SLOTS, PAD), 0)
        keyb_ref[...] = jnp.where(slot < lengths[seq], -running_sum(forget, False), NEG)

    lane = lax.broadcasted_iota(jnp.int32, (SLOTS, wide), 1)
    lane_all = lax.broadcasted_iota(jnp.int32, (SLOTS, PAD), 1)
    queries = q_ref[...].astype(F32)
    keys = k_ref[...].astype(F32)
    values_t = jnp.transpose(v_ref[...].astype(F32)).astype(BF16)
    allowed = causal(BLOCK)
    sides = []
    for head in range(per_group):
        spare = HEAD if head == 0 else 0
        bias = pick_lane(keyb_ref[...], lane_all, group * per_group + head)
        sides.append(
            (key_side(keys, bias, lane, head, spare), query_side(queries, lane, head, spare))
        )
    for start in range(0, SLOTS, BLOCK):
        stop = start + BLOCK
        outs = []
        for head in range(per_group):
            key_aug, query_aug = sides[head]
            picked = query_aug[start:stop]
            diag = jnp.where(allowed, dot_nt(key_aug[start:stop], picked), NEG)
            top = jnp.max(diag, axis=0, keepdims=True)
            if start:
                early = dot_nt(key_aug[:start], picked)
                top = jnp.maximum(top, jnp.max(early, axis=0, keepdims=True))
            diag = jnp.exp(diag - top)
            total = jnp.sum(diag, axis=0, keepdims=True)
            value_rows = values_t[head * HEAD : (head + 1) * HEAD]
            out = dot_nn(value_rows[:, start:stop], diag.astype(BF16))
            if start:
                early = jnp.exp(early - top)
                total = total + jnp.sum(early, axis=0, keepdims=True)
                out = out + dot_nn(value_rows[:, :start], early.astype(BF16))
            outs.append(out / total)
            shift_ref[pl.ds(group * per_group + head, 1), start:stop] = -(top + jnp.log(total))
        block = jnp.transpose(jnp.concatenate(outs, axis=0))
        att_ref[start:stop] = block.astype(BF16)
        gated_ref[start:stop] = (block * jax.nn.sigmoid(gate_ref[start:stop])).astype(BF16)


def attend_back_body(
    q_ref, k_ref, v_ref, gate_ref, att_ref, grad_ref, logit_ref, bias_ref, shift_ref, keyb_ref,
    out_ref, bias_out_ref, low_ref, dk_ref, dv_ref, row_ref, col_ref,
    *, per_group, groups,
):
    group = pl.program_id(1)
    wide = per_group * HEAD
    part = groups * wide

    def columns(which):
        if groups == 1:
            return slice(which * part, which * part + wide)
        return pl.ds(pl.multiple_of(which * part + group * wide, wide), wide)

    @pl.when(group == 0)
    def _():
        row_ref[...] = jnp.zeros(row_ref.shape, F32)
        col_ref[...] = jnp.zeros(col_ref.shape, F32)

    lane = lax.broadcasted_iota(jnp.int32, (SLOTS, wide), 1)
    lane_all = lax.broadcasted_iota(jnp.int32, (SLOTS, PAD), 1)
    sig = jax.nn.sigmoid(gate_ref[...])
    grad_gated = grad_ref[...].astype(F32)
    grad_att = grad_gated * sig
    out_ref[:, columns(3)] = (grad_att * att_ref[...].astype(F32) * (1.0 - sig)).astype(BF16)
    low_ref[...] = grad_att.astype(BF16)
    queries = q_ref[...].astype(F32)
    keys = k_ref[...].astype(F32)
    keys_t = jnp.transpose(keys).astype(BF16)
    ones = jnp.ones((16, SLOTS), BF16)
    allowed = causal(BLOCK)
    grad_low = low_ref[...].astype(F32)
    sides = []
    for head in range(per_group):
        spare = HEAD if head == 0 else 0
        bias = pick_lane(keyb_ref[...], lane_all, group * per_group + head)
        sides.append(
            (
                key_side(keys, bias, lane, head, spare),
                query_side(queries, lane, head, spare),
                jnp.where(head_span(lane, head), grad_low, 0.0).astype(BF16),
                jnp.concatenate([keys_t[head * HEAD : (head + 1) * HEAD], ones], axis=0),
            )
        )
    for start in reversed(range(0, SLOTS, BLOCK)):
        stop = start + BLOCK
        last = stop == SLOTS
        outs = []
        for head in range(per_group):
            key_aug, query_aug, grad_own, key_rows = sides[head]
            picked = query_aug[start:stop]
            grads = grad_own[start:stop]
            shift = shift_ref[pl.ds(group * per_group + head, 1), start:stop]
            spans = [(start, stop)] + ([(0, start)] if start else [])
            weights = []
            inner = jnp.zeros((1, BLOCK), F32)
            for low, high in spans:
                score = dot_nt(key_aug[low:high], picked) + shift
                if low == start:
                    score = jnp.where(allowed, score, NEG)
                soft = jnp.exp(score)
                grad_soft = dot_nt(v_ref[low:high], grads)
                inner = inner + jnp.sum(soft * grad_soft, axis=0, keepdims=True)
                weights.append((soft, grad_soft))
            out = jnp.zeros((HEAD + 16, BLOCK), F32)
            for (low, high), (soft, grad_soft) in zip(spans, weights):
                grad_score = (soft * (grad_soft - inner)).astype(BF16)
                key_part = dot_nn(grad_score, picked)
                value_part = dot_nn(soft.astype(BF16), grads)
                if last:
                    dk_ref[head, low:high] = key_part
                    if head == 0:
                        dv_ref[low:high] = value_part
                    else:
                        dv_ref[low:high] += value_part
                else:
                    dk_ref[head, low:high] += key_part
                    dv_ref[low:high] += value_part
                out = out + dot_nn(key_rows[:, low:high], grad_score)
            outs.append(out[:HEAD] * HEAD ** (-0.5))
            row_ref[pl.ds(group * per_group + head, 1), start:stop] = out[HEAD : HEAD + 1]
        out_ref[start:stop, columns(0)] = jnp.transpose(jnp.concatenate(outs, axis=0)).astype(BF16)
    grad_keys = dk_ref[0]
    for head in range(per_group):
        spare = HEAD if head == 0 else 0
        found = dk_ref[head]
        if head:
            grad_keys = jnp.where(head_span(lane, head), found, grad_keys)
        sums = pick_lane(found, lane, spare)
        col_ref[...] = jnp.where(lane_all == group * per_group + head, sums, col_ref[...])
    out_ref[:, columns(1)] = grad_keys.astype(BF16)
    out_ref[:, columns(2)] = dv_ref[...].astype(BF16)

    @pl.when(group == groups - 1)
    def _():
        grad_decay = jnp.transpose(row_ref[...]) - col_ref[...]
        logit = logit_ref[...] + bias_ref[0:1]
        grad_logit = running_sum(grad_decay, True) * jax.nn.sigmoid(-logit)
        out_ref[:, 4 * part :] = grad_logit.astype(BF16)
        bias_out_ref[...] = jnp.broadcast_to(jnp.sum(grad_logit, axis=0, keepdims=True), (8, PAD))


def head_blocks(part):
    heads = part // HEAD
    per_group = 2 if heads % 2 == 0 else heads
    groups = heads // per_group
    wide = per_group * HEAD

    def of(array, which, count):
        if part % 128 == 0:
            return array, pl.BlockSpec((SLOTS, wide), lambda s, g: (s, which * groups + g))
        return (
            array[:, which * part : (which + 1) * part],
            pl.BlockSpec((SLOTS, wide), lambda s, g: (s, g)),
        )

    return per_group, groups, wide, of


def logit_block(gate_logit, part):
    if part % PAD == 0:
        return gate_logit, pl.BlockSpec((SLOTS, PAD), lambda s, g: (s, part // PAD))
    return gate_logit[:, part:], pl.BlockSpec((SLOTS, PAD), lambda s, g: (s, 0))


def attend(proj, gate_logit, bias_rows, lengths, part):
    rows = proj.shape[0]
    seqs = rows // SLOTS
    per_group, groups, wide, of = head_blocks(part)
    fix = lambda f: (lambda s, g, lengths: f(s, g))
    parts = [of(proj, 0, 3), of(proj, 1, 3), of(proj, 2, 3), of(gate_logit, 0, 1)]
    parts.append(logit_block(gate_logit, part))
    parts.append((bias_rows, pl.BlockSpec((8, PAD), lambda s, g: (0, 0))))
    wide_spec = pl.BlockSpec((SLOTS, wide), lambda s, g: (s, g))
    outs = [
        (jax.ShapeDtypeStruct((rows, part), BF16), wide_spec),
        (jax.ShapeDtypeStruct((rows, part), BF16), wide_spec),
        (jax.ShapeDtypeStruct((seqs * PAD, SLOTS), F32), pl.BlockSpec((PAD, SLOTS), lambda s, g: (s, 0))),
        (jax.ShapeDtypeStruct((rows, PAD), F32), pl.BlockSpec((SLOTS, PAD), lambda s, g: (s, 0))),
    ]
    respec = lambda spec: pl.BlockSpec(spec.block_shape, fix(spec.index_map))
    return pl.pallas_call(
        functools.partial(attend_body, per_group=per_group),
        out_shape=[shape for shape, _ in outs],
        grid_spec=pltpu.PrefetchScalarGridSpec(
            num_scalar_prefetch=1,
            grid=(seqs, groups),
            in_specs=[respec(spec) for _, spec in parts],
            out_specs=[respec(spec) for _, spec in outs],
        ),
        compiler_params=pltpu.CompilerParams(
            dimension_semantics=("arbitrary", "arbitrary"), vmem_limit_bytes=48 * 2**20
        ),
        name="attend",
    )(lengths, *[array for array, _ in parts])


def attend_back(proj, gate_logit, attended, grad_gated, bias_rows, shift, keyb, part):
    rows = proj.shape[0]
    seqs = rows // SLOTS
    per_group, groups, wide, of = head_blocks(part)
    parts = [of(proj, 0, 3), of(proj, 1, 3), of(proj, 2, 3), of(gate_logit, 0, 1)]
    parts += [of(attended, 0, 1), of(grad_gated, 0, 1)]
    parts.append(logit_block(gate_logit, part))
    parts.append((bias_rows, pl.BlockSpec((8, PAD), lambda s, g: (0, 0))))
    parts.append((shift, pl.BlockSpec((PAD, SLOTS), lambda s, g: (s, 0))))
    parts.append((keyb, pl.BlockSpec((SLOTS, PAD), lambda s, g: (s, 0))))
    total = 4 * part + PAD
    return pl.pallas_call(
        functools.partial(attend_back_body, per_group=per_group, groups=groups),
        out_shape=[
            jax.ShapeDtypeStruct((rows, total), BF16),
            jax.ShapeDtypeStruct((seqs * 8, PAD), F32),
        ],
        grid=(seqs, groups),
        in_specs=[spec for _, spec in parts],
        out_specs=[
            pl.BlockSpec((SLOTS, total), lambda s, g: (s, 0)),
            pl.BlockSpec((8, PAD), lambda s, g: (s, 0)),
        ],
        scratch_shapes=[
            pltpu.VMEM((SLOTS, wide), BF16),
            pltpu.VMEM((per_group, SLOTS, wide), F32),
            pltpu.VMEM((SLOTS, wide), F32),
            pltpu.VMEM((PAD, SLOTS), F32),
            pltpu.VMEM((SLOTS, PAD), F32),
        ],
        compiler_params=pltpu.CompilerParams(
            dimension_semantics=("arbitrary", "arbitrary"), vmem_limit_bytes=56 * 2**20
        ),
        name="attend_back",
    )(*[array for array, _ in parts])


def on_device(
    layer_input,
    gain_attn,
    w_attn,
    w_forget,
    forget_bias,
    w_out,
    gain_mlp,
    w_mlp,
    w_down,
    lengths,
    cotangent,
):
    own_rows, width = layer_input.shape
    group_seqs = lengths.shape[0]
    group_rows = group_seqs * SLOTS
    part = w_attn.shape[2]
    heads_dev = part // HEAD
    units = w_mlp.shape[2]
    own_d = w_attn.shape[0]
    tensor_index = lax.axis_index("tensor")
    bias_own = lax.dynamic_slice_in_dim(forget_bias, tensor_index * heads_dev, heads_dev)
    positions = tensor_index * own_rows + jnp.arange(own_rows, dtype=jnp.int32)
    seq_of_row = positions // SLOTS
    matches = seq_of_row[:, None] == jnp.arange(group_seqs, dtype=jnp.int32)[None, :]
    own_lengths = jnp.sum(jnp.where(matches, lengths[None, :], 0), axis=1)
    valid = (positions % SLOTS < own_lengths).astype(F32)[:, None]

    attn_shard = jnp.concatenate(
        [w_attn.reshape(own_d, 4 * part), jnp.pad(w_forget, ((0, 0), (0, PAD - heads_dev)))], axis=1
    )
    attn_cols = 4 * part + PAD
    first_full = gather_dp(jnp.concatenate([attn_shard, w_out.T], axis=1))
    second_shard = jnp.concatenate([w_down.T, w_mlp.reshape(own_d, 2 * units)], axis=1)
    first_full, second_shard = hold(first_full, second_shard)
    second_full = gather_dp(second_shard)
    attn_full, out_full = (first_full[:, :attn_cols], first_full[:, attn_cols:])
    down_full, mlp_full = (second_full[:, :units], second_full[:, units:])

    input_wide = layer_input.astype(F32)
    scaled_attn, inverse_attn = norm_parts(input_wide)
    normed_all = share_rows((scaled_attn * gain_attn).astype(BF16))
    grad_final = cotangent.astype(F32) * valid
    normed_all, grad_final_all = hold(normed_all, share_rows(grad_final.astype(BF16)))

    proj = dot_nn(normed_all, attn_full[:, : 3 * part]).astype(BF16)
    gate_logit = dot_nn(normed_all, attn_full[:, 3 * part :])
    bias_rows = jnp.broadcast_to(jnp.pad(bias_own, (0, PAD - heads_dev))[None, :], (8, PAD))
    gated, attended, shift, keyb = attend(proj, gate_logit, bias_rows, lengths, part)

    def attn_term(first_row, row_count):
        return dot_nt(lax.dynamic_slice_in_dim(gated, first_row, row_count), out_full)

    leaving, staying = term_parts(attn_term, own_rows)
    arrived, staying = hold(cross(leaving), staying)
    middle = input_wide + (staying + arrived.astype(F32))
    scaled_mlp, inverse_mlp = norm_parts(middle)
    normed_mid = share_rows((scaled_mlp * gain_mlp).astype(BF16))
    grad_hidden = dot_nn(grad_final_all, down_full)
    gate_pre = dot_nn(normed_mid, mlp_full[:, :units])
    up_pre = dot_nn(normed_mid, mlp_full[:, units:])
    gate_s = jax.nn.sigmoid(gate_pre)
    silu = gate_pre * gate_s
    hidden = (silu * up_pre).astype(BF16)
    grad_gate = (grad_hidden * up_pre * gate_s * (1.0 + gate_pre * (1.0 - gate_s))).astype(BF16)
    grad_up = (grad_hidden * silu).astype(BF16)
    grad_pair = jnp.concatenate([grad_gate, grad_up], axis=1)

    def mlp_back_term(first_row, row_count):
        return dot_nt(lax.dynamic_slice_in_dim(grad_pair, first_row, row_count), mlp_full)

    down_grad = dot_tn(grad_final_all, hidden).astype(BF16)
    down_part = scatter_dp(down_grad)
    leaving, staying = term_parts(mlp_back_term, own_rows)
    mlp_grad = dot_tn(normed_mid, grad_pair).astype(BF16)
    arrived, staying, mlp_grad = hold(cross(leaving), staying, mlp_grad)
    mlp_part = scatter_dp(mlp_grad)
    grad_normed_mlp = staying + arrived.astype(F32)

    gain_mlp_part = jnp.sum(scaled_mlp * grad_normed_mlp, axis=0)
    grad_middle = grad_final + norm_back(grad_normed_mlp, scaled_mlp, inverse_mlp, gain_mlp)
    grad_middle_low, hidden = hold(grad_middle.astype(BF16), hidden)

    def mlp_term(first_row, row_count):
        return dot_nt(lax.dynamic_slice_in_dim(hidden, first_row, row_count), down_full)

    leaving, staying = term_parts(mlp_term, own_rows)
    grad_branch_all, leaving, staying = hold(share_rows(grad_middle_low), leaving, staying)
    arrived_out = cross(leaving)

    grad_gated = dot_nn(grad_branch_all, out_full).astype(BF16)
    grad_proj, bias_sums = attend_back(
        proj, gate_logit, attended, grad_gated, bias_rows, shift, keyb, part
    )
    grad_proj, arrived_out = hold(grad_proj, arrived_out)
    layer_output = (valid * (middle + (staying + arrived_out.astype(F32)))).astype(BF16)
    bias_part = jnp.sum(bias_sums.reshape(group_seqs, 8, PAD)[:, 0, :heads_dev], axis=0)
    def attn_back_term(first_row, row_count):
        return dot_nt(lax.dynamic_slice_in_dim(grad_proj, first_row, row_count), attn_full)

    first_grad = jnp.concatenate(
        [dot_tn(normed_all, grad_proj), dot_tn(grad_branch_all, gated)], axis=1
    ).astype(BF16)
    first_part = scatter_dp(first_grad)
    leaving, staying = term_parts(attn_back_term, own_rows)
    grad_normed_attn = staying + cross(leaving).astype(F32)
    attn_part, out_part = (first_part[:, :attn_cols], first_part[:, attn_cols:])
    gain_attn_part = jnp.sum(scaled_attn * grad_normed_attn, axis=0)
    grad_input = grad_middle + norm_back(grad_normed_attn, scaled_attn, inverse_attn, gain_attn)
    bias_full = lax.dynamic_update_slice_in_dim(
        jnp.zeros(forget_bias.shape, F32), bias_part, tensor_index * heads_dev, 0
    )
    grad_gain_attn, grad_gain_mlp, grad_forget_bias = lax.psum(
        (gain_attn_part, gain_mlp_part, bias_full), ("dp", "tensor")
    )
    attn_part = attn_part.astype(F32)
    return (
        layer_output,
        grad_input,
        grad_gain_attn,
        attn_part[:, : 4 * part].reshape(own_d, 4, part),
        attn_part[:, 4 * part : 4 * part + heads_dev],
        grad_forget_bias,
        out_part.astype(F32).T,
        grad_gain_mlp,
        mlp_part.astype(F32).reshape(own_d, 2, units),
        down_part.astype(F32).T,
    )


def solution(mesh):
    placed = (
        P(("dp", "tensor"), None),
        P(),
        P("dp", None, "tensor"),
        P("dp", "tensor"),
        P(),
        P("tensor", "dp"),
        P(),
        P("dp", None, "tensor"),
        P("tensor", "dp"),
        P("dp"),
        P(("dp", "tensor"), None),
    )
    return jax.shard_map(
        on_device,
        mesh=mesh,
        in_specs=placed,
        out_specs=(
            P(("dp", "tensor"), None),
            P(("dp", "tensor"), None),
            P(),
            P("dp", None, "tensor"),
            P("dp", "tensor"),
            P(),
            P("tensor", "dp"),
            P(),
            P("dp", None, "tensor"),
            P("tensor", "dp"),
        ),
        check_vma=False,
    )
```

```python
import functools

import jax
import jax.numpy as jnp
from jax import lax
from jax.experimental import pallas as pl
from jax.experimental.pallas import tpu as pltpu
from jax.sharding import PartitionSpec as P

HEAD = 64
SLOTS = 1024
EPS = 1e-06
PAD = 128
BLOCK = 256
NEG = -1e30

BF16 = jnp.bfloat16
F32 = jnp.float32


def norm_parts(rows):
    inverse = lax.rsqrt(jnp.mean(rows * rows, axis=-1, keepdims=True) + EPS)
    return (rows * inverse, inverse)


def norm_back(grad_normed, scaled, inverse, gain):
    grad_scaled = grad_normed * gain
    inner_sum = jnp.mean(grad_scaled * scaled, axis=-1, keepdims=True)
    return inverse * (grad_scaled - scaled * inner_sum)


def dot_nn(a, b):
    return lax.dot_general(a, b, (((1,), (0,)), ((), ())), preferred_element_type=F32)


def dot_nt(a, b):
    return lax.dot_general(a, b, (((1,), (1,)), ((), ())), preferred_element_type=F32)


def dot_tn(a, b):
    return lax.dot_general(a, b, (((0,), (0,)), ((), ())), preferred_element_type=F32)


def swap(rows):
    return lax.ppermute(rows, "tensor", [(0, 1), (1, 0)])


def share_rows(own):
    if lax.axis_size("tensor") != 2:
        return lax.all_gather(own, "tensor", axis=0, tiled=True)
    other = swap(own)
    first = lax.axis_index("tensor") == 0
    return jnp.concatenate([jnp.where(first, own, other), jnp.where(first, other, own)], axis=0)


def hold(*values):
    return lax.optimization_barrier(values)


def term_parts(term_fn, own_rows):
    size = lax.axis_size("tensor")
    if size != 2:
        return (term_fn(jnp.int32(0), own_rows * size).astype(BF16), jnp.zeros((), F32))
    index = lax.axis_index("tensor")
    return (
        term_fn((1 - index) * own_rows, own_rows).astype(BF16),
        term_fn(index * own_rows, own_rows),
    )


def cross(leaving):
    if lax.axis_size("tensor") != 2:
        return lax.psum_scatter(leaving, "tensor", scatter_dimension=0, tiled=True)
    return swap(leaving)


def gather_dp(shard):
    return lax.all_gather(shard, "dp", axis=0, tiled=True)


def scatter_dp(grad):
    return lax.psum_scatter(grad, "dp", scatter_dimension=0, tiled=True)


def trade(value, axis, mask):
    size = lax.axis_size(axis)
    return lax.ppermute(value, axis, [(i, i ^ mask) for i in range(size)])


def take(array, axis, index):
    return lax.dynamic_index_in_dim(array, index, axis, keepdims=False)


def scatter_links(first, second, beside):
    size = lax.axis_size("dp")
    if size % 4 or size & (size - 1):
        return (scatter_dp(first).astype(F32), scatter_dp(second).astype(F32), beside)
    layers = size // 4
    index = lax.axis_index("dp")
    core, side, layer = (index % 2, index // 2 % 2, index // 4)

    def over_core(grad):
        grad = grad.reshape(layers, 2, 2, grad.shape[0] // size, grad.shape[1])
        arrived = trade(take(grad, 2, 1 - core), "dp", 1)
        return (take(grad, 2, core).astype(F32) + arrived.astype(F32)).astype(BF16)

    def side_pieces(grad, axis):
        return [take(grad, axis, side), trade(take(grad, axis, 1 - side), "dp", 2)]

    def layer_pieces(grad):
        sent = [trade(take(grad, 0, layer ^ k), "dp", 4 * k) for k in range(1, layers)]
        return [take(grad, 0, layer), *sent]

    def total(pieces):
        result = pieces[0].astype(F32)
        for piece in pieces[1:]:
            result = result + piece.astype(F32)
        return result

    first, second = hold(over_core(first), over_core(second))
    first, second, beside = hold(side_pieces(first, 1), layer_pieces(second), beside)
    first, second = hold(total(first).astype(BF16), total(second).astype(BF16))
    return (total(layer_pieces(first)), total(side_pieces(second, 0)), beside)


def sum_all(value):
    for axis in ("dp", "tensor"):
        size = lax.axis_size(axis)
        if size & (size - 1):
            value = lax.psum(value, axis)
            continue
        step = 1
        while step < size:
            value = value + trade(value, axis, step)
            step *= 2
    return value


def head_span(lane, head):
    return (lane >= head * HEAD) & (lane < (head + 1) * HEAD)


def key_side(keys, bias, lane, head, spare):
    high = bias.astype(BF16).astype(F32)
    rest = bias - high
    mid = rest.astype(BF16).astype(F32)
    extra = jnp.where(
        lane == spare,
        high,
        jnp.where(lane == spare + 1, mid, jnp.where(lane == spare + 2, rest - mid, 0.0)),
    )
    return jnp.where(head_span(lane, head), keys, extra).astype(BF16)


def query_side(queries, lane, head, spare):
    ones = jnp.where((lane >= spare) & (lane < spare + 3), 1.0, 0.0)
    return jnp.where(head_span(lane, head), queries * HEAD ** (-0.5), ones).astype(BF16)


def pick_lane(rows, lane, index):
    return jnp.sum(jnp.where(lane == index, rows, 0.0), axis=1, keepdims=True)


def running_sum(rows, reverse):
    step = 1
    while step < SLOTS:
        zeros = jnp.zeros((step, rows.shape[1]), F32)
        if reverse:
            moved = jnp.concatenate([rows[step:], zeros], axis=0)
        else:
            moved = jnp.concatenate([zeros, rows[:-step]], axis=0)
        rows = rows + moved
        step *= 2
    return rows


def causal(block):
    key = lax.broadcasted_iota(jnp.int32, (block, block), 0)
    query = lax.broadcasted_iota(jnp.int32, (block, block), 1)
    return key <= query


def attend_body(
    lengths, q_ref, k_ref, v_ref, gate_ref, logit_ref, bias_ref, gated_ref, att_ref, shift_ref, keyb_ref,
    *, per_group,
):
    seq = pl.program_id(0)
    group = pl.program_id(1)
    wide = per_group * HEAD

    @pl.when(group == 0)
    def _():
        logit = logit_ref[...] + bias_ref[0:1]
        forget = jnp.minimum(logit, 0.0) - jnp.log1p(jnp.exp(-jnp.abs(logit)))
        slot = lax.broadcasted_iota(jnp.int32, (SLOTS, PAD), 0)
        keyb_ref[...] = jnp.where(slot < lengths[seq], -running_sum(forget, False), NEG)

    lane = lax.broadcasted_iota(jnp.int32, (SLOTS, wide), 1)
    lane_all = lax.broadcasted_iota(jnp.int32, (SLOTS, PAD), 1)
    queries = q_ref[...].astype(F32)
    keys = k_ref[...].astype(F32)
    values_t = jnp.transpose(v_ref[...].astype(F32)).astype(BF16)
    allowed = causal(BLOCK)
    sides = []
    for head in range(per_group):
        spare = HEAD if head == 0 else 0
        bias = pick_lane(keyb_ref[...], lane_all, group * per_group + head)
        sides.append(
            (key_side(keys, bias, lane, head, spare), query_side(queries, lane, head, spare))
        )
    for start in range(0, SLOTS, BLOCK):
        stop = start + BLOCK
        outs = []
        for head in range(per_group):
            key_aug, query_aug = sides[head]
            picked = query_aug[start:stop]
            diag = jnp.where(allowed, dot_nt(key_aug[start:stop], picked), NEG)
            top = jnp.max(diag, axis=0, keepdims=True)
            if start:
                early = dot_nt(key_aug[:start], picked)
                top = jnp.maximum(top, jnp.max(early, axis=0, keepdims=True))
            diag = jnp.exp(diag - top)
            total = jnp.sum(diag, axis=0, keepdims=True)
            value_rows = values_t[head * HEAD : (head + 1) * HEAD]
            out = dot_nn(value_rows[:, start:stop], diag.astype(BF16))
            if start:
                early = jnp.exp(early - top)
                total = total + jnp.sum(early, axis=0, keepdims=True)
                out = out + dot_nn(value_rows[:, :start], early.astype(BF16))
            outs.append(out / total)
            shift_ref[pl.ds(group * per_group + head, 1), start:stop] = -(top + jnp.log(total))
        block = jnp.transpose(jnp.concatenate(outs, axis=0))
        att_ref[start:stop] = block.astype(BF16)
        gated_ref[start:stop] = (block * jax.nn.sigmoid(gate_ref[start:stop])).astype(BF16)


def attend_back_body(
    q_ref, k_ref, v_ref, gate_ref, att_ref, grad_ref, logit_ref, bias_ref, shift_ref, keyb_ref,
    out_ref, bias_out_ref, low_ref, dk_ref, dv_ref, row_ref, col_ref,
    *, per_group, groups,
):
    group = pl.program_id(1)
    wide = per_group * HEAD
    part = groups * wide

    def columns(which):
        first = which * part + (PAD if which == 3 else 0)
        if groups == 1:
            return slice(first, first + wide)
        return pl.ds(pl.multiple_of(first + group * wide, wide), wide)

    @pl.when(group == 0)
    def _():
        row_ref[...] = jnp.zeros(row_ref.shape, F32)
        col_ref[...] = jnp.zeros(col_ref.shape, F32)

    lane = lax.broadcasted_iota(jnp.int32, (SLOTS, wide), 1)
    lane_all = lax.broadcasted_iota(jnp.int32, (SLOTS, PAD), 1)
    sig = jax.nn.sigmoid(gate_ref[...])
    grad_gated = grad_ref[...].astype(F32)
    grad_att = grad_gated * sig
    out_ref[:, columns(3)] = (grad_att * att_ref[...].astype(F32) * (1.0 - sig)).astype(BF16)
    low_ref[...] = grad_att.astype(BF16)
    queries = q_ref[...].astype(F32)
    keys = k_ref[...].astype(F32)
    keys_t = jnp.transpose(keys).astype(BF16)
    ones = jnp.ones((16, SLOTS), BF16)
    allowed = causal(BLOCK)
    grad_low = low_ref[...].astype(F32)
    sides = []
    for head in range(per_group):
        spare = HEAD if head == 0 else 0
        bias = pick_lane(keyb_ref[...], lane_all, group * per_group + head)
        sides.append(
            (
                key_side(keys, bias, lane, head, spare),
                query_side(queries, lane, head, spare),
                jnp.where(head_span(lane, head), grad_low, 0.0).astype(BF16),
                jnp.concatenate([keys_t[head * HEAD : (head + 1) * HEAD], ones], axis=0),
            )
        )
    for start in reversed(range(0, SLOTS, BLOCK)):
        stop = start + BLOCK
        last = stop == SLOTS
        outs = []
        for head in range(per_group):
            key_aug, query_aug, grad_own, key_rows = sides[head]
            picked = query_aug[start:stop]
            grads = grad_own[start:stop]
            shift = shift_ref[pl.ds(group * per_group + head, 1), start:stop]
            spans = [(start, stop)] + ([(0, start)] if start else [])
            weights = []
            inner = jnp.zeros((1, BLOCK), F32)
            for low, high in spans:
                score = dot_nt(key_aug[low:high], picked) + shift
                if low == start:
                    score = jnp.where(allowed, score, NEG)
                soft = jnp.exp(score)
                grad_soft = dot_nt(v_ref[low:high], grads)
                inner = inner + jnp.sum(soft * grad_soft, axis=0, keepdims=True)
                weights.append((soft, grad_soft))
            out = jnp.zeros((HEAD + 16, BLOCK), F32)
            for (low, high), (soft, grad_soft) in zip(spans, weights):
                grad_score = (soft * (grad_soft - inner)).astype(BF16)
                key_part = dot_nn(grad_score, picked)
                value_part = dot_nn(soft.astype(BF16), grads)
                if last:
                    dk_ref[head, low:high] = key_part
                    if head == 0:
                        dv_ref[low:high] = value_part
                    else:
                        dv_ref[low:high] += value_part
                else:
                    dk_ref[head, low:high] += key_part
                    dv_ref[low:high] += value_part
                out = out + dot_nn(key_rows[:, low:high], grad_score)
            outs.append(out[:HEAD] * HEAD ** (-0.5))
            row_ref[pl.ds(group * per_group + head, 1), start:stop] = out[HEAD : HEAD + 1]
        out_ref[start:stop, columns(0)] = jnp.transpose(jnp.concatenate(outs, axis=0)).astype(BF16)
    grad_keys = dk_ref[0]
    for head in range(per_group):
        spare = HEAD if head == 0 else 0
        found = dk_ref[head]
        if head:
            grad_keys = jnp.where(head_span(lane, head), found, grad_keys)
        sums = pick_lane(found, lane, spare)
        col_ref[...] = jnp.where(lane_all == group * per_group + head, sums, col_ref[...])
    out_ref[:, columns(1)] = grad_keys.astype(BF16)
    out_ref[:, columns(2)] = dv_ref[...].astype(BF16)

    @pl.when(group == groups - 1)
    def _():
        grad_decay = jnp.transpose(row_ref[...]) - col_ref[...]
        logit = logit_ref[...] + bias_ref[0:1]
        grad_logit = running_sum(grad_decay, True) * jax.nn.sigmoid(-logit)
        out_ref[:, 3 * part : 3 * part + PAD] = grad_logit.astype(BF16)
        bias_out_ref[...] = jnp.broadcast_to(jnp.sum(grad_logit, axis=0, keepdims=True), (8, PAD))


def head_blocks(part):
    heads = part // HEAD
    per_group = 2 if heads % 2 == 0 else heads
    groups = heads // per_group
    wide = per_group * HEAD

    def of(array, which, count):
        if part % 128 == 0:
            return array, pl.BlockSpec((SLOTS, wide), lambda s, g: (s, which * groups + g))
        return (
            array[:, which * part : (which + 1) * part],
            pl.BlockSpec((SLOTS, wide), lambda s, g: (s, g)),
        )

    return per_group, groups, wide, of


def logit_block(gate_logit):
    return gate_logit, pl.BlockSpec((SLOTS, PAD), lambda s, g: (s, 0))


def gate_block(gate_logit, part, wide):
    if part % 128 == 0:
        return gate_logit, pl.BlockSpec((SLOTS, wide), lambda s, g: (s, g + PAD // wide))
    return gate_logit[:, PAD:], pl.BlockSpec((SLOTS, wide), lambda s, g: (s, g))


def attend(proj, gate_logit, bias_rows, lengths, part):
    rows = proj.shape[0]
    seqs = rows // SLOTS
    per_group, groups, wide, of = head_blocks(part)
    fix = lambda f: (lambda s, g, lengths: f(s, g))
    parts = [of(proj, 0, 3), of(proj, 1, 3), of(proj, 2, 3), gate_block(gate_logit, part, wide)]
    parts.append(logit_block(gate_logit))
    parts.append((bias_rows, pl.BlockSpec((8, PAD), lambda s, g: (0, 0))))
    wide_spec = pl.BlockSpec((SLOTS, wide), lambda s, g: (s, g))
    outs = [
        (jax.ShapeDtypeStruct((rows, part), BF16), wide_spec),
        (jax.ShapeDtypeStruct((rows, part), BF16), wide_spec),
        (jax.ShapeDtypeStruct((seqs * PAD, SLOTS), F32), pl.BlockSpec((PAD, SLOTS), lambda s, g: (s, 0))),
        (jax.ShapeDtypeStruct((rows, PAD), F32), pl.BlockSpec((SLOTS, PAD), lambda s, g: (s, 0))),
    ]
    respec = lambda spec: pl.BlockSpec(spec.block_shape, fix(spec.index_map))
    return pl.pallas_call(
        functools.partial(attend_body, per_group=per_group),
        out_shape=[shape for shape, _ in outs],
        grid_spec=pltpu.PrefetchScalarGridSpec(
            num_scalar_prefetch=1,
            grid=(seqs, groups),
            in_specs=[respec(spec) for _, spec in parts],
            out_specs=[respec(spec) for _, spec in outs],
        ),
        compiler_params=pltpu.CompilerParams(
            dimension_semantics=("arbitrary", "arbitrary"), vmem_limit_bytes=48 * 2**20
        ),
        name="attend",
    )(lengths, *[array for array, _ in parts])


def attend_back(proj, gate_logit, attended, grad_gated, bias_rows, shift, keyb, part):
    rows = proj.shape[0]
    seqs = rows // SLOTS
    per_group, groups, wide, of = head_blocks(part)
    parts = [of(proj, 0, 3), of(proj, 1, 3), of(proj, 2, 3), gate_block(gate_logit, part, wide)]
    parts += [of(attended, 0, 1), of(grad_gated, 0, 1)]
    parts.append(logit_block(gate_logit))
    parts.append((bias_rows, pl.BlockSpec((8, PAD), lambda s, g: (0, 0))))
    parts.append((shift, pl.BlockSpec((PAD, SLOTS), lambda s, g: (s, 0))))
    parts.append((keyb, pl.BlockSpec((SLOTS, PAD), lambda s, g: (s, 0))))
    total = 4 * part + PAD
    return pl.pallas_call(
        functools.partial(attend_back_body, per_group=per_group, groups=groups),
        out_shape=[
            jax.ShapeDtypeStruct((rows, total), BF16),
            jax.ShapeDtypeStruct((seqs * 8, PAD), F32),
        ],
        grid=(seqs, groups),
        in_specs=[spec for _, spec in parts],
        out_specs=[
            pl.BlockSpec((SLOTS, total), lambda s, g: (s, 0)),
            pl.BlockSpec((8, PAD), lambda s, g: (s, 0)),
        ],
        scratch_shapes=[
            pltpu.VMEM((SLOTS, wide), BF16),
            pltpu.VMEM((per_group, SLOTS, wide), F32),
            pltpu.VMEM((SLOTS, wide), F32),
            pltpu.VMEM((PAD, SLOTS), F32),
            pltpu.VMEM((SLOTS, PAD), F32),
        ],
        compiler_params=pltpu.CompilerParams(
            dimension_semantics=("arbitrary", "arbitrary"), vmem_limit_bytes=56 * 2**20
        ),
        name="attend_back",
    )(*[array for array, _ in parts])


def on_device(
    layer_input,
    gain_attn,
    w_attn,
    w_forget,
    forget_bias,
    w_out,
    gain_mlp,
    w_mlp,
    w_down,
    lengths,
    cotangent,
):
    own_rows, width = layer_input.shape
    group_seqs = lengths.shape[0]
    group_rows = group_seqs * SLOTS
    part = w_attn.shape[2]
    heads_dev = part // HEAD
    units = w_mlp.shape[2]
    own_d = w_attn.shape[0]
    tensor_index = lax.axis_index("tensor")
    bias_own = lax.dynamic_slice_in_dim(forget_bias, tensor_index * heads_dev, heads_dev)
    positions = tensor_index * own_rows + jnp.arange(own_rows, dtype=jnp.int32)
    seq_of_row = positions // SLOTS
    matches = seq_of_row[:, None] == jnp.arange(group_seqs, dtype=jnp.int32)[None, :]
    own_lengths = jnp.sum(jnp.where(matches, lengths[None, :], 0), axis=1)
    valid = (positions % SLOTS < own_lengths).astype(F32)[:, None]

    attn_shard = jnp.concatenate(
        [
            w_attn[:, :3].reshape(own_d, 3 * part),
            jnp.pad(w_forget, ((0, 0), (0, PAD - heads_dev))),
            w_attn[:, 3],
        ],
        axis=1,
    )
    attn_cols = 4 * part + PAD
    first_full = gather_dp(jnp.concatenate([attn_shard, w_out.T], axis=1))
    second_shard = jnp.concatenate([w_down.T, w_mlp.reshape(own_d, 2 * units)], axis=1)
    input_wide = layer_input.astype(F32)
    scaled_attn, inverse_attn = norm_parts(input_wide)
    normed_all = share_rows((scaled_attn * gain_attn).astype(BF16))
    grad_final = cotangent.astype(F32) * valid
    grad_final_all = share_rows(grad_final.astype(BF16))
    first_full, second_shard, normed_all, grad_final_all = hold(
        first_full, second_shard, normed_all, grad_final_all
    )
    second_full = gather_dp(second_shard)
    attn_full, out_full = (first_full[:, :attn_cols], first_full[:, attn_cols:])
    down_full, mlp_full = (second_full[:, :units], second_full[:, units:])

    proj = dot_nn(normed_all, attn_full[:, : 3 * part]).astype(BF16)
    gate_logit = dot_nn(normed_all, attn_full[:, 3 * part :])
    bias_rows = jnp.broadcast_to(jnp.pad(bias_own, (0, PAD - heads_dev))[None, :], (8, PAD))
    gated, attended, shift, keyb = attend(proj, gate_logit, bias_rows, lengths, part)

    def attn_term(first_row, row_count):
        return dot_nt(lax.dynamic_slice_in_dim(gated, first_row, row_count), out_full)

    leaving, staying = term_parts(attn_term, own_rows)
    arrived, staying = hold(cross(leaving), staying)
    middle = input_wide + (staying + arrived.astype(F32))
    scaled_mlp, inverse_mlp = norm_parts(middle)
    normed_mid = share_rows((scaled_mlp * gain_mlp).astype(BF16))
    grad_hidden = dot_nn(grad_final_all, down_full)
    gate_pre = dot_nn(normed_mid, mlp_full[:, :units])
    up_pre = dot_nn(normed_mid, mlp_full[:, units:])
    gate_s = jax.nn.sigmoid(gate_pre)
    silu = gate_pre * gate_s
    hidden = (silu * up_pre).astype(BF16)
    grad_gate = (grad_hidden * up_pre * gate_s * (1.0 + gate_pre * (1.0 - gate_s))).astype(BF16)
    grad_up = (grad_hidden * silu).astype(BF16)
    grad_pair = jnp.concatenate([grad_gate, grad_up], axis=1)

    def mlp_back_term(first_row, row_count):
        return dot_nt(lax.dynamic_slice_in_dim(grad_pair, first_row, row_count), mlp_full)

    down_grad = dot_tn(grad_final_all, hidden).astype(BF16)
    down_part = scatter_dp(down_grad)
    leaving, staying = term_parts(mlp_back_term, own_rows)
    mlp_grad = dot_tn(normed_mid, grad_pair).astype(BF16)
    arrived, staying, mlp_grad = hold(cross(leaving), staying, mlp_grad)
    mlp_part = scatter_dp(mlp_grad)
    grad_normed_mlp = staying + arrived.astype(F32)

    gain_mlp_part = jnp.sum(scaled_mlp * grad_normed_mlp, axis=0)
    grad_middle = grad_final + norm_back(grad_normed_mlp, scaled_mlp, inverse_mlp, gain_mlp)
    grad_middle_low, hidden = hold(grad_middle.astype(BF16), hidden)

    def mlp_term(first_row, row_count):
        return dot_nt(lax.dynamic_slice_in_dim(hidden, first_row, row_count), down_full)

    leaving, staying = term_parts(mlp_term, own_rows)
    grad_branch_all, leaving, staying = hold(share_rows(grad_middle_low), leaving, staying)
    arrived_out = cross(leaving)

    grad_gated = dot_nn(grad_branch_all, out_full).astype(BF16)
    grad_proj, bias_sums = attend_back(
        proj, gate_logit, attended, grad_gated, bias_rows, shift, keyb, part
    )
    grad_proj, arrived_out = hold(grad_proj, arrived_out)
    layer_output = (valid * (middle + (staying + arrived_out.astype(F32)))).astype(BF16)
    bias_part = jnp.sum(bias_sums.reshape(group_seqs, 8, PAD)[:, 0, :heads_dev], axis=0)
    def attn_back_term(first_row, row_count):
        return dot_nt(lax.dynamic_slice_in_dim(grad_proj, first_row, row_count), attn_full)

    leaving, staying = term_parts(attn_back_term, own_rows)
    arrived_back = cross(leaving)
    main_grad = dot_tn(normed_all, grad_proj[:, : 3 * part + PAD]).astype(BF16)
    rest_grad = jnp.concatenate(
        [
            dot_tn(normed_all, grad_proj[:, 3 * part + PAD :]).astype(BF16),
            dot_tn(grad_branch_all, gated).astype(BF16),
        ],
        axis=1,
    )
    main_part, rest_part, arrived_back = scatter_links(main_grad, rest_grad, arrived_back)
    grad_normed_attn = staying + arrived_back.astype(F32)
    gain_attn_part = jnp.sum(scaled_attn * grad_normed_attn, axis=0)
    grad_input = grad_middle + norm_back(grad_normed_attn, scaled_attn, inverse_attn, gain_attn)
    bias_full = lax.dynamic_update_slice_in_dim(
        jnp.zeros(forget_bias.shape, F32), bias_part, tensor_index * heads_dev, 0
    )
    heads = forget_bias.shape[0]
    sums = sum_all(
        jnp.concatenate(
            [gain_attn_part, gain_mlp_part, jnp.pad(bias_full, (0, -heads % 128))]
        ).reshape(-1, 128)
    ).reshape(-1)
    return (
        layer_output,
        grad_input,
        sums[:width],
        jnp.concatenate([main_part[:, : 3 * part], rest_part[:, :part]], axis=1).reshape(
            own_d, 4, part
        ),
        main_part[:, 3 * part : 3 * part + heads_dev],
        sums[2 * width : 2 * width + heads],
        rest_part[:, part:].T,
        sums[width : 2 * width],
        mlp_part.astype(F32).reshape(own_d, 2, units),
        down_part.astype(F32).T,
    )


def solution(mesh):
    placed = (
        P(("dp", "tensor"), None),
        P(),
        P("dp", None, "tensor"),
        P("dp", "tensor"),
        P(),
        P("tensor", "dp"),
        P(),
        P("dp", None, "tensor"),
        P("tensor", "dp"),
        P("dp"),
        P(("dp", "tensor"), None),
    )
    return jax.shard_map(
        on_device,
        mesh=mesh,
        in_specs=placed,
        out_specs=(
            P(("dp", "tensor"), None),
            P(("dp", "tensor"), None),
            P(),
            P("dp", None, "tensor"),
            P("dp", "tensor"),
            P(),
            P("tensor", "dp"),
            P(),
            P("dp", None, "tensor"),
            P("tensor", "dp"),
        ),
        check_vma=False,
    )
```

```python
import functools

import jax
import jax.numpy as jnp
from jax import lax
from jax.experimental import pallas as pl
from jax.experimental.pallas import tpu as pltpu
from jax.sharding import PartitionSpec as P

HEAD = 64
SLOTS = 1024
EPS = 1e-06
PAD = 128
BLOCK = 256
NEG = -1e30

BF16 = jnp.bfloat16
F32 = jnp.float32


def norm_parts(rows):
    inverse = lax.rsqrt(jnp.mean(rows * rows, axis=-1, keepdims=True) + EPS)
    return (rows * inverse, inverse)


def norm_back(grad_normed, scaled, inverse, gain):
    grad_scaled = grad_normed * gain
    inner_sum = jnp.mean(grad_scaled * scaled, axis=-1, keepdims=True)
    return inverse * (grad_scaled - scaled * inner_sum)


def dot_nn(a, b):
    return lax.dot_general(a, b, (((1,), (0,)), ((), ())), preferred_element_type=F32)


def dot_nt(a, b):
    return lax.dot_general(a, b, (((1,), (1,)), ((), ())), preferred_element_type=F32)


def dot_tn(a, b):
    return lax.dot_general(a, b, (((0,), (0,)), ((), ())), preferred_element_type=F32)


def swap(rows):
    return lax.ppermute(rows, "tensor", [(0, 1), (1, 0)])


def share_rows(own):
    if lax.axis_size("tensor") != 2:
        return lax.all_gather(own, "tensor", axis=0, tiled=True)
    other = swap(own)
    first = lax.axis_index("tensor") == 0
    return jnp.concatenate([jnp.where(first, own, other), jnp.where(first, other, own)], axis=0)


def hold(*values):
    return lax.optimization_barrier(values)


def term_parts(term_fn, own_rows):
    size = lax.axis_size("tensor")
    if size != 2:
        return (term_fn(jnp.int32(0), own_rows * size).astype(BF16), jnp.zeros((), F32))
    index = lax.axis_index("tensor")
    return (
        term_fn((1 - index) * own_rows, own_rows).astype(BF16),
        term_fn(index * own_rows, own_rows),
    )


def cross(leaving):
    if lax.axis_size("tensor") != 2:
        return lax.psum_scatter(leaving, "tensor", scatter_dimension=0, tiled=True)
    return swap(leaving)


def gather_dp(shard):
    return lax.all_gather(shard, "dp", axis=0, tiled=True)


def scatter_dp(grad):
    return lax.psum_scatter(grad, "dp", scatter_dimension=0, tiled=True)


def trade(value, axis, mask):
    size = lax.axis_size(axis)
    return lax.ppermute(value, axis, [(i, i ^ mask) for i in range(size)])


def take(array, axis, index):
    return lax.dynamic_index_in_dim(array, index, axis, keepdims=False)


def over_core(grad):
    size = lax.axis_size("dp")
    core = lax.axis_index("dp") % 2
    grad = grad.reshape(size // 4, 2, 2, grad.shape[0] // size, grad.shape[1])
    arrived = trade(take(grad, 2, 1 - core), "dp", 1)
    return (take(grad, 2, core).astype(F32) + arrived.astype(F32)).astype(BF16)


def side_pieces(grad, axis):
    side = lax.axis_index("dp") // 2 % 2
    return [take(grad, axis, side), trade(take(grad, axis, 1 - side), "dp", 2)]


def layer_pieces(grad):
    layer = lax.axis_index("dp") // 4
    sent = [trade(take(grad, 0, layer ^ k), "dp", 4 * k) for k in range(1, grad.shape[0])]
    return [take(grad, 0, layer), *sent]


def total(pieces):
    result = pieces[0].astype(F32)
    for piece in pieces[1:]:
        result = result + piece.astype(F32)
    return result


def add_traded(value, axis, masks):
    for mask in masks:
        value = value + trade(value, axis, mask)
    return value


def masks_of(size):
    return [1 << k for k in range(size.bit_length() - 1)]


def head_span(lane, head):
    return (lane >= head * HEAD) & (lane < (head + 1) * HEAD)


def key_side(keys, bias, lane, head, spare):
    high = bias.astype(BF16).astype(F32)
    rest = bias - high
    mid = rest.astype(BF16).astype(F32)
    extra = jnp.where(
        lane == spare,
        high,
        jnp.where(lane == spare + 1, mid, jnp.where(lane == spare + 2, rest - mid, 0.0)),
    )
    return jnp.where(head_span(lane, head), keys, extra).astype(BF16)


def query_side(queries, lane, head, spare):
    ones = jnp.where((lane >= spare) & (lane < spare + 3), 1.0, 0.0)
    return jnp.where(head_span(lane, head), queries * HEAD ** (-0.5), ones).astype(BF16)


def pick_lane(rows, lane, index):
    return jnp.sum(jnp.where(lane == index, rows, 0.0), axis=1, keepdims=True)


def running_sum(rows, reverse):
    step = 1
    while step < SLOTS:
        zeros = jnp.zeros((step, rows.shape[1]), F32)
        if reverse:
            moved = jnp.concatenate([rows[step:], zeros], axis=0)
        else:
            moved = jnp.concatenate([zeros, rows[:-step]], axis=0)
        rows = rows + moved
        step *= 2
    return rows


def causal(block):
    key = lax.broadcasted_iota(jnp.int32, (block, block), 0)
    query = lax.broadcasted_iota(jnp.int32, (block, block), 1)
    return key <= query


def attend_body(
    lengths, q_ref, k_ref, v_ref, gate_ref, logit_ref, bias_ref, gated_ref, att_ref, shift_ref, keyb_ref,
    *, per_group,
):
    seq = pl.program_id(0)
    group = pl.program_id(1)
    wide = per_group * HEAD

    @pl.when(group == 0)
    def _():
        logit = logit_ref[...] + bias_ref[0:1]
        forget = jnp.minimum(logit, 0.0) - jnp.log1p(jnp.exp(-jnp.abs(logit)))
        slot = lax.broadcasted_iota(jnp.int32, (SLOTS, PAD), 0)
        keyb_ref[...] = jnp.where(slot < lengths[seq], -running_sum(forget, False), NEG)

    lane = lax.broadcasted_iota(jnp.int32, (SLOTS, wide), 1)
    lane_all = lax.broadcasted_iota(jnp.int32, (SLOTS, PAD), 1)
    queries = q_ref[...].astype(F32)
    keys = k_ref[...].astype(F32)
    values_t = jnp.transpose(v_ref[...].astype(F32)).astype(BF16)
    allowed = causal(BLOCK)
    sides = []
    for head in range(per_group):
        spare = HEAD if head == 0 else 0
        bias = pick_lane(keyb_ref[...], lane_all, group * per_group + head)
        sides.append(
            (key_side(keys, bias, lane, head, spare), query_side(queries, lane, head, spare))
        )
    for start in range(0, SLOTS, BLOCK):
        stop = start + BLOCK
        outs = []
        for head in range(per_group):
            key_aug, query_aug = sides[head]
            picked = query_aug[start:stop]
            diag = jnp.where(allowed, dot_nt(key_aug[start:stop], picked), NEG)
            top = jnp.max(diag, axis=0, keepdims=True)
            if start:
                early = dot_nt(key_aug[:start], picked)
                top = jnp.maximum(top, jnp.max(early, axis=0, keepdims=True))
            diag = jnp.exp(diag - top)
            total = jnp.sum(diag, axis=0, keepdims=True)
            value_rows = values_t[head * HEAD : (head + 1) * HEAD]
            out = dot_nn(value_rows[:, start:stop], diag.astype(BF16))
            if start:
                early = jnp.exp(early - top)
                total = total + jnp.sum(early, axis=0, keepdims=True)
                out = out + dot_nn(value_rows[:, :start], early.astype(BF16))
            outs.append(out / total)
            shift_ref[pl.ds(group * per_group + head, 1), start:stop] = -(top + jnp.log(total))
        block = jnp.transpose(jnp.concatenate(outs, axis=0))
        att_ref[start:stop] = block.astype(BF16)
        gated_ref[start:stop] = (block * jax.nn.sigmoid(gate_ref[start:stop])).astype(BF16)


def attend_back_body(
    q_ref, k_ref, v_ref, gate_ref, att_ref, grad_ref, logit_ref, bias_ref, shift_ref, keyb_ref,
    out_ref, bias_out_ref, low_ref, dk_ref, dv_ref, row_ref, col_ref,
    *, per_group, groups,
):
    group = pl.program_id(1)
    wide = per_group * HEAD
    part = groups * wide

    def columns(which):
        first = which * part + (PAD if which == 3 else 0)
        if groups == 1:
            return slice(first, first + wide)
        return pl.ds(pl.multiple_of(first + group * wide, wide), wide)

    @pl.when(group == 0)
    def _():
        row_ref[...] = jnp.zeros(row_ref.shape, F32)
        col_ref[...] = jnp.zeros(col_ref.shape, F32)

    lane = lax.broadcasted_iota(jnp.int32, (SLOTS, wide), 1)
    lane_all = lax.broadcasted_iota(jnp.int32, (SLOTS, PAD), 1)
    sig = jax.nn.sigmoid(gate_ref[...])
    grad_gated = grad_ref[...].astype(F32)
    grad_att = grad_gated * sig
    out_ref[:, columns(3)] = (grad_att * att_ref[...].astype(F32) * (1.0 - sig)).astype(BF16)
    low_ref[...] = grad_att.astype(BF16)
    queries = q_ref[...].astype(F32)
    keys = k_ref[...].astype(F32)
    keys_t = jnp.transpose(keys).astype(BF16)
    ones = jnp.ones((16, SLOTS), BF16)
    allowed = causal(BLOCK)
    grad_low = low_ref[...].astype(F32)
    sides = []
    for head in range(per_group):
        spare = HEAD if head == 0 else 0
        bias = pick_lane(keyb_ref[...], lane_all, group * per_group + head)
        sides.append(
            (
                key_side(keys, bias, lane, head, spare),
                query_side(queries, lane, head, spare),
                jnp.where(head_span(lane, head), grad_low, 0.0).astype(BF16),
                jnp.concatenate([keys_t[head * HEAD : (head + 1) * HEAD], ones], axis=0),
            )
        )
    for start in reversed(range(0, SLOTS, BLOCK)):
        stop = start + BLOCK
        last = stop == SLOTS
        outs = []
        for head in range(per_group):
            key_aug, query_aug, grad_own, key_rows = sides[head]
            picked = query_aug[start:stop]
            grads = grad_own[start:stop]
            shift = shift_ref[pl.ds(group * per_group + head, 1), start:stop]
            spans = [(start, stop)] + ([(0, start)] if start else [])
            weights = []
            inner = jnp.zeros((1, BLOCK), F32)
            for low, high in spans:
                score = dot_nt(key_aug[low:high], picked) + shift
                if low == start:
                    score = jnp.where(allowed, score, NEG)
                soft = jnp.exp(score)
                grad_soft = dot_nt(v_ref[low:high], grads)
                inner = inner + jnp.sum(soft * grad_soft, axis=0, keepdims=True)
                weights.append((soft, grad_soft))
            out = jnp.zeros((HEAD + 16, BLOCK), F32)
            for (low, high), (soft, grad_soft) in zip(spans, weights):
                grad_score = (soft * (grad_soft - inner)).astype(BF16)
                key_part = dot_nn(grad_score, picked)
                value_part = dot_nn(soft.astype(BF16), grads)
                if last:
                    dk_ref[head, low:high] = key_part
                    if head == 0:
                        dv_ref[low:high] = value_part
                    else:
                        dv_ref[low:high] += value_part
                else:
                    dk_ref[head, low:high] += key_part
                    dv_ref[low:high] += value_part
                out = out + dot_nn(key_rows[:, low:high], grad_score)
            outs.append(out[:HEAD] * HEAD ** (-0.5))
            row_ref[pl.ds(group * per_group + head, 1), start:stop] = out[HEAD : HEAD + 1]
        out_ref[start:stop, columns(0)] = jnp.transpose(jnp.concatenate(outs, axis=0)).astype(BF16)
    grad_keys = dk_ref[0]
    for head in range(per_group):
        spare = HEAD if head == 0 else 0
        found = dk_ref[head]
        if head:
            grad_keys = jnp.where(head_span(lane, head), found, grad_keys)
        sums = pick_lane(found, lane, spare)
        col_ref[...] = jnp.where(lane_all == group * per_group + head, sums, col_ref[...])
    out_ref[:, columns(1)] = grad_keys.astype(BF16)
    out_ref[:, columns(2)] = dv_ref[...].astype(BF16)

    @pl.when(group == groups - 1)
    def _():
        grad_decay = jnp.transpose(row_ref[...]) - col_ref[...]
        logit = logit_ref[...] + bias_ref[0:1]
        grad_logit = running_sum(grad_decay, True) * jax.nn.sigmoid(-logit)
        out_ref[:, 3 * part : 3 * part + PAD] = grad_logit.astype(BF16)
        bias_out_ref[...] = jnp.broadcast_to(jnp.sum(grad_logit, axis=0, keepdims=True), (8, PAD))


def head_blocks(part):
    heads = part // HEAD
    per_group = 2 if heads % 2 == 0 else heads
    groups = heads // per_group
    wide = per_group * HEAD

    def of(array, which, count):
        if part % 128 == 0:
            return array, pl.BlockSpec((SLOTS, wide), lambda s, g: (s, which * groups + g))
        return (
            array[:, which * part : (which + 1) * part],
            pl.BlockSpec((SLOTS, wide), lambda s, g: (s, g)),
        )

    return per_group, groups, wide, of


def logit_block(gate_logit):
    return gate_logit, pl.BlockSpec((SLOTS, PAD), lambda s, g: (s, 0))


def gate_block(gate_logit, part, wide):
    if part % 128 == 0:
        return gate_logit, pl.BlockSpec((SLOTS, wide), lambda s, g: (s, g + PAD // wide))
    return gate_logit[:, PAD:], pl.BlockSpec((SLOTS, wide), lambda s, g: (s, g))


def attend(proj, gate_logit, bias_rows, lengths, part):
    rows = proj.shape[0]
    seqs = rows // SLOTS
    per_group, groups, wide, of = head_blocks(part)
    fix = lambda f: (lambda s, g, lengths: f(s, g))
    parts = [of(proj, 0, 3), of(proj, 1, 3), of(proj, 2, 3), gate_block(gate_logit, part, wide)]
    parts.append(logit_block(gate_logit))
    parts.append((bias_rows, pl.BlockSpec((8, PAD), lambda s, g: (0, 0))))
    wide_spec = pl.BlockSpec((SLOTS, wide), lambda s, g: (s, g))
    outs = [
        (jax.ShapeDtypeStruct((rows, part), BF16), wide_spec),
        (jax.ShapeDtypeStruct((rows, part), BF16), wide_spec),
        (jax.ShapeDtypeStruct((seqs * PAD, SLOTS), F32), pl.BlockSpec((PAD, SLOTS), lambda s, g: (s, 0))),
        (jax.ShapeDtypeStruct((rows, PAD), F32), pl.BlockSpec((SLOTS, PAD), lambda s, g: (s, 0))),
    ]
    respec = lambda spec: pl.BlockSpec(spec.block_shape, fix(spec.index_map))
    return pl.pallas_call(
        functools.partial(attend_body, per_group=per_group),
        out_shape=[shape for shape, _ in outs],
        grid_spec=pltpu.PrefetchScalarGridSpec(
            num_scalar_prefetch=1,
            grid=(seqs, groups),
            in_specs=[respec(spec) for _, spec in parts],
            out_specs=[respec(spec) for _, spec in outs],
        ),
        compiler_params=pltpu.CompilerParams(
            dimension_semantics=("arbitrary", "arbitrary"), vmem_limit_bytes=48 * 2**20
        ),
        name="attend",
    )(lengths, *[array for array, _ in parts])


def attend_back(proj, gate_logit, attended, grad_gated, bias_rows, shift, keyb, part):
    rows = proj.shape[0]
    seqs = rows // SLOTS
    per_group, groups, wide, of = head_blocks(part)
    parts = [of(proj, 0, 3), of(proj, 1, 3), of(proj, 2, 3), gate_block(gate_logit, part, wide)]
    parts += [of(attended, 0, 1), of(grad_gated, 0, 1)]
    parts.append(logit_block(gate_logit))
    parts.append((bias_rows, pl.BlockSpec((8, PAD), lambda s, g: (0, 0))))
    parts.append((shift, pl.BlockSpec((PAD, SLOTS), lambda s, g: (s, 0))))
    parts.append((keyb, pl.BlockSpec((SLOTS, PAD), lambda s, g: (s, 0))))
    total = 4 * part + PAD
    return pl.pallas_call(
        functools.partial(attend_back_body, per_group=per_group, groups=groups),
        out_shape=[
            jax.ShapeDtypeStruct((rows, total), BF16),
            jax.ShapeDtypeStruct((seqs * 8, PAD), F32),
        ],
        grid=(seqs, groups),
        in_specs=[spec for _, spec in parts],
        out_specs=[
            pl.BlockSpec((SLOTS, total), lambda s, g: (s, 0)),
            pl.BlockSpec((8, PAD), lambda s, g: (s, 0)),
        ],
        scratch_shapes=[
            pltpu.VMEM((SLOTS, wide), BF16),
            pltpu.VMEM((per_group, SLOTS, wide), F32),
            pltpu.VMEM((SLOTS, wide), F32),
            pltpu.VMEM((PAD, SLOTS), F32),
            pltpu.VMEM((SLOTS, PAD), F32),
        ],
        compiler_params=pltpu.CompilerParams(
            dimension_semantics=("arbitrary", "arbitrary"), vmem_limit_bytes=56 * 2**20
        ),
        name="attend_back",
    )(*[array for array, _ in parts])


def on_device(
    layer_input,
    gain_attn,
    w_attn,
    w_forget,
    forget_bias,
    w_out,
    gain_mlp,
    w_mlp,
    w_down,
    lengths,
    cotangent,
):
    own_rows, width = layer_input.shape
    group_seqs = lengths.shape[0]
    part = w_attn.shape[2]
    heads_dev = part // HEAD
    units = w_mlp.shape[2]
    own_d = w_attn.shape[0]
    tensor_index = lax.axis_index("tensor")
    bias_own = lax.dynamic_slice_in_dim(forget_bias, tensor_index * heads_dev, heads_dev)
    positions = tensor_index * own_rows + jnp.arange(own_rows, dtype=jnp.int32)
    seq_of_row = positions // SLOTS
    matches = seq_of_row[:, None] == jnp.arange(group_seqs, dtype=jnp.int32)[None, :]
    own_lengths = jnp.sum(jnp.where(matches, lengths[None, :], 0), axis=1)
    valid = (positions % SLOTS < own_lengths).astype(F32)[:, None]

    attn_shard = jnp.concatenate(
        [
            w_attn[:, :3].reshape(own_d, 3 * part),
            jnp.pad(w_forget, ((0, 0), (0, PAD - heads_dev))),
            w_attn[:, 3],
        ],
        axis=1,
    )
    attn_cols = 4 * part + PAD
    first_full = gather_dp(jnp.concatenate([attn_shard, w_out.T], axis=1))
    second_shard = jnp.concatenate([w_down.T, w_mlp.reshape(own_d, 2 * units)], axis=1)
    input_wide = layer_input.astype(F32)
    scaled_attn, inverse_attn = norm_parts(input_wide)
    normed_all = share_rows((scaled_attn * gain_attn).astype(BF16))
    grad_final = cotangent.astype(F32) * valid
    grad_final_all = share_rows(grad_final.astype(BF16))
    first_full, second_shard, normed_all, grad_final_all = hold(
        first_full, second_shard, normed_all, grad_final_all
    )
    second_full = gather_dp(second_shard)
    attn_full, out_full = (first_full[:, :attn_cols], first_full[:, attn_cols:])
    down_full, mlp_full = (second_full[:, :units], second_full[:, units:])

    proj = dot_nn(normed_all, attn_full[:, : 3 * part]).astype(BF16)
    gate_logit = dot_nn(normed_all, attn_full[:, 3 * part :])
    bias_rows = jnp.broadcast_to(jnp.pad(bias_own, (0, PAD - heads_dev))[None, :], (8, PAD))
    gated, attended, shift, keyb = attend(proj, gate_logit, bias_rows, lengths, part)

    def attn_term(first_row, row_count):
        return dot_nt(lax.dynamic_slice_in_dim(gated, first_row, row_count), out_full)

    leaving, staying = term_parts(attn_term, own_rows)
    arrived, staying = hold(cross(leaving), staying)
    middle = input_wide + (staying + arrived.astype(F32))
    scaled_mlp, inverse_mlp = norm_parts(middle)
    normed_mid = share_rows((scaled_mlp * gain_mlp).astype(BF16))
    grad_hidden = dot_nn(grad_final_all, down_full)
    normed_mid, grad_hidden = hold(normed_mid, grad_hidden)
    gate_pre = dot_nn(normed_mid, mlp_full[:, :units])
    up_pre = dot_nn(normed_mid, mlp_full[:, units:])
    gate_s = jax.nn.sigmoid(gate_pre)
    silu = gate_pre * gate_s
    hidden = (silu * up_pre).astype(BF16)
    grad_gate = (grad_hidden * up_pre * gate_s * (1.0 + gate_pre * (1.0 - gate_s))).astype(BF16)
    grad_up = (grad_hidden * silu).astype(BF16)
    grad_pair = jnp.concatenate([grad_gate, grad_up], axis=1)

    def mlp_back_term(first_row, row_count):
        return dot_nt(lax.dynamic_slice_in_dim(grad_pair, first_row, row_count), mlp_full)

    down_grad = dot_tn(grad_final_all, hidden).astype(BF16)
    down_part = scatter_dp(down_grad)
    leaving, staying = term_parts(mlp_back_term, own_rows)
    mlp_grad = dot_tn(normed_mid, grad_pair).astype(BF16)
    arrived, staying, mlp_grad = hold(cross(leaving), staying, mlp_grad)
    mlp_part = scatter_dp(mlp_grad)
    grad_normed_mlp = staying + arrived.astype(F32)

    gain_mlp_part = jnp.sum(scaled_mlp * grad_normed_mlp, axis=0)
    grad_middle = grad_final + norm_back(grad_normed_mlp, scaled_mlp, inverse_mlp, gain_mlp)
    grad_middle_low, hidden = hold(grad_middle.astype(BF16), hidden)

    def mlp_term(first_row, row_count):
        return dot_nt(lax.dynamic_slice_in_dim(hidden, first_row, row_count), down_full)

    leaving, staying = term_parts(mlp_term, own_rows)
    grad_branch_all, leaving, staying = hold(share_rows(grad_middle_low), leaving, staying)
    arrived_out = cross(leaving)

    grad_gated = dot_nn(grad_branch_all, out_full).astype(BF16)
    grad_proj, bias_sums = attend_back(
        proj, gate_logit, attended, grad_gated, bias_rows, shift, keyb, part
    )
    grad_proj, arrived_out = hold(grad_proj, arrived_out)
    layer_output = (valid * (middle + (staying + arrived_out.astype(F32)))).astype(BF16)
    bias_part = jnp.sum(bias_sums.reshape(group_seqs, 8, PAD)[:, 0, :heads_dev], axis=0)

    def attn_back_term(first_row, row_count):
        return dot_nt(lax.dynamic_slice_in_dim(grad_proj, first_row, row_count), attn_full)

    bias_full = lax.dynamic_update_slice_in_dim(
        jnp.zeros(forget_bias.shape, F32), bias_part, tensor_index * heads_dev, 0
    )
    heads = forget_bias.shape[0]

    def finish(arrived):
        grad_normed_attn = staying + arrived.astype(F32)
        grad_input = grad_middle + norm_back(grad_normed_attn, scaled_attn, inverse_attn, gain_attn)
        terms = [jnp.sum(scaled_attn * grad_normed_attn, axis=0), gain_mlp_part]
        terms.append(jnp.pad(bias_full, (0, -heads % 128)))
        return grad_input, jnp.concatenate(terms).reshape(-1, 128)

    leaving, staying = term_parts(attn_back_term, own_rows)
    leaving, grad_later = hold(leaving, grad_proj)
    arrived_back = cross(leaving)
    main_grad = dot_tn(normed_all, grad_later[:, : 3 * part + PAD]).astype(BF16)
    gate_grad = dot_tn(normed_all, grad_later[:, 3 * part + PAD :]).astype(BF16)
    size = lax.axis_size("dp")
    tensor_size = lax.axis_size("tensor")
    if size % 4 or size & (size - 1) or tensor_size & (tensor_size - 1):
        main_part, gate_part = (scatter_dp(main_grad).astype(F32), scatter_dp(gate_grad).astype(F32))
        out_part = scatter_dp(dot_tn(grad_branch_all, gated).astype(BF16))
        grad_input, sums = finish(arrived_back)
        sums = lax.psum(sums, ("dp", "tensor"))
    else:
        out_grad = dot_tn(grad_branch_all, gated).astype(BF16)
        main_half, gate_half, out_half, arrived_back = hold(
            over_core(main_grad), over_core(gate_grad), over_core(out_grad), arrived_back
        )
        rest_half = jnp.concatenate([gate_half, out_half], axis=-1)
        grad_input, sums = finish(arrived_back)
        sums = add_traded(sums, "dp", [1])
        sums = add_traded(sums, "tensor", masks_of(tensor_size))
        main_half, rest_half, sums = hold(side_pieces(main_half, 1), layer_pieces(rest_half), sums)
        sums = add_traded(sums, "dp", masks_of(size)[2:])
        main_half, rest_half, sums = hold(
            total(main_half).astype(BF16), total(rest_half).astype(BF16), sums
        )
        main_part, rest_part = (total(layer_pieces(main_half)), total(side_pieces(rest_half, 0)))
        gate_part, out_part = (rest_part[:, :part], rest_part[:, part:])
        sums = add_traded(sums, "dp", [2])
    sums = sums.reshape(-1)
    return (
        layer_output,
        grad_input,
        sums[:width],
        jnp.concatenate([main_part[:, : 3 * part], gate_part], axis=1).reshape(
            own_d, 4, part
        ),
        main_part[:, 3 * part : 3 * part + heads_dev],
        sums[2 * width : 2 * width + heads],
        out_part.astype(F32).T,
        sums[width : 2 * width],
        mlp_part.astype(F32).reshape(own_d, 2, units),
        down_part.astype(F32).T,
    )


def solution(mesh):
    placed = (
        P(("dp", "tensor"), None),
        P(),
        P("dp", None, "tensor"),
        P("dp", "tensor"),
        P(),
        P("tensor", "dp"),
        P(),
        P("dp", None, "tensor"),
        P("tensor", "dp"),
        P("dp"),
        P(("dp", "tensor"), None),
    )

    return jax.shard_map(
        on_device,
        mesh=mesh,
        in_specs=placed,
        out_specs=(
            P(("dp", "tensor"), None),
            P(("dp", "tensor"), None),
            P(),
            P("dp", None, "tensor"),
            P("dp", "tensor"),
            P(),
            P("tensor", "dp"),
            P(),
            P("dp", None, "tensor"),
            P("tensor", "dp"),
        ),
        check_vma=False,
    )
```

```python
import functools

import jax
import jax.numpy as jnp
from jax import lax
from jax.experimental import pallas as pl
from jax.experimental.pallas import tpu as pltpu
from jax.sharding import PartitionSpec as P

HEAD = 64
SLOTS = 1024
EPS = 1e-06
PAD = 128
BLOCK = 256
NEG = -1e30

BF16 = jnp.bfloat16
F32 = jnp.float32


def norm_parts(rows):
    inverse = lax.rsqrt(jnp.mean(rows * rows, axis=-1, keepdims=True) + EPS)
    return (rows * inverse, inverse)


def norm_back(grad_normed, scaled, inverse, gain):
    grad_scaled = grad_normed * gain
    inner_sum = jnp.mean(grad_scaled * scaled, axis=-1, keepdims=True)
    return inverse * (grad_scaled - scaled * inner_sum)


def dot_nn(a, b):
    return lax.dot_general(a, b, (((1,), (0,)), ((), ())), preferred_element_type=F32)


def dot_nt(a, b):
    return lax.dot_general(a, b, (((1,), (1,)), ((), ())), preferred_element_type=F32)


def dot_tn(a, b):
    return lax.dot_general(a, b, (((0,), (0,)), ((), ())), preferred_element_type=F32)


def swap(rows):
    return lax.ppermute(rows, "tensor", [(0, 1), (1, 0)])


def share_rows(own):
    if lax.axis_size("tensor") != 2:
        return lax.all_gather(own, "tensor", axis=0, tiled=True)
    other = swap(own)
    first = lax.axis_index("tensor") == 0
    return jnp.concatenate([jnp.where(first, own, other), jnp.where(first, other, own)], axis=0)


def hold(*values):
    return lax.optimization_barrier(values)


def term_parts(term_fn, own_rows):
    size = lax.axis_size("tensor")
    if size != 2:
        return (term_fn(jnp.int32(0), own_rows * size).astype(BF16), jnp.zeros((), F32))
    index = lax.axis_index("tensor")
    return (
        term_fn((1 - index) * own_rows, own_rows).astype(BF16),
        term_fn(index * own_rows, own_rows),
    )


def cross(leaving):
    if lax.axis_size("tensor") != 2:
        return lax.psum_scatter(leaving, "tensor", scatter_dimension=0, tiled=True)
    return swap(leaving)


def gather_dp(shard):
    return lax.all_gather(shard, "dp", axis=0, tiled=True)


def scatter_dp(grad):
    return lax.psum_scatter(grad, "dp", scatter_dimension=0, tiled=True)


def trade(value, axis, mask):
    size = lax.axis_size(axis)
    return lax.ppermute(value, axis, [(i, i ^ mask) for i in range(size)])


def take(array, axis, index):
    return lax.dynamic_index_in_dim(array, index, axis, keepdims=False)


def over_core(grad):
    size = lax.axis_size("dp")
    core = lax.axis_index("dp") % 2
    grad = grad.reshape(size // 4, 2, 2, grad.shape[0] // size, grad.shape[1])
    arrived = trade(take(grad, 2, 1 - core), "dp", 1)
    return (take(grad, 2, core).astype(F32) + arrived.astype(F32)).astype(BF16)


def side_pieces(grad, axis):
    side = lax.axis_index("dp") // 2 % 2
    return [take(grad, axis, side), trade(take(grad, axis, 1 - side), "dp", 2)]


def layer_pieces(grad):
    layer = lax.axis_index("dp") // 4
    sent = [trade(take(grad, 0, layer ^ k), "dp", 4 * k) for k in range(1, grad.shape[0])]
    return [take(grad, 0, layer), *sent]


def total(pieces):
    result = pieces[0].astype(F32)
    for piece in pieces[1:]:
        result = result + piece.astype(F32)
    return result


def add_traded(value, axis, masks):
    for mask in masks:
        value = value + trade(value, axis, mask)
    return value


def masks_of(size):
    return [1 << k for k in range(size.bit_length() - 1)]


def head_span(lane, head):
    return (lane >= head * HEAD) & (lane < (head + 1) * HEAD)


def key_side(keys, bias, lane, head, spare):
    high = bias.astype(BF16).astype(F32)
    rest = bias - high
    mid = rest.astype(BF16).astype(F32)
    extra = jnp.where(
        lane == spare,
        high,
        jnp.where(lane == spare + 1, mid, jnp.where(lane == spare + 2, rest - mid, 0.0)),
    )
    return jnp.where(head_span(lane, head), keys, extra).astype(BF16)


def query_side(queries, lane, head, spare):
    ones = jnp.where((lane >= spare) & (lane < spare + 3), 1.0, 0.0)
    return jnp.where(head_span(lane, head), queries * HEAD ** (-0.5), ones).astype(BF16)


def pick_lane(rows, lane, index):
    return jnp.sum(jnp.where(lane == index, rows, 0.0), axis=1, keepdims=True)


def running_sum(rows, reverse):
    step = 1
    while step < SLOTS:
        zeros = jnp.zeros((step, rows.shape[1]), F32)
        if reverse:
            moved = jnp.concatenate([rows[step:], zeros], axis=0)
        else:
            moved = jnp.concatenate([zeros, rows[:-step]], axis=0)
        rows = rows + moved
        step *= 2
    return rows


def causal(block):
    key = lax.broadcasted_iota(jnp.int32, (block, block), 0)
    query = lax.broadcasted_iota(jnp.int32, (block, block), 1)
    return key <= query


def attend_body(
    lengths, q_ref, k_ref, v_ref, gate_ref, logit_ref, bias_ref, gated_ref, att_ref, shift_ref, keyb_ref,
    *, per_group,
):
    seq = pl.program_id(0)
    group = pl.program_id(1)
    wide = per_group * HEAD

    @pl.when(group == 0)
    def _():
        logit = logit_ref[...] + bias_ref[0:1]
        forget = jnp.minimum(logit, 0.0) - jnp.log1p(jnp.exp(-jnp.abs(logit)))
        slot = lax.broadcasted_iota(jnp.int32, (SLOTS, PAD), 0)
        keyb_ref[...] = jnp.where(slot < lengths[seq], -running_sum(forget, False), NEG)

    lane = lax.broadcasted_iota(jnp.int32, (SLOTS, wide), 1)
    lane_all = lax.broadcasted_iota(jnp.int32, (SLOTS, PAD), 1)
    queries = q_ref[...].astype(F32)
    keys = k_ref[...].astype(F32)
    values_t = jnp.transpose(v_ref[...].astype(F32)).astype(BF16)
    allowed = causal(BLOCK)
    sides = []
    for head in range(per_group):
        spare = HEAD if head == 0 else 0
        bias = pick_lane(keyb_ref[...], lane_all, group * per_group + head)
        sides.append(
            (key_side(keys, bias, lane, head, spare), query_side(queries, lane, head, spare))
        )
    for start in range(0, SLOTS, BLOCK):
        stop = start + BLOCK
        outs = []
        for head in range(per_group):
            key_aug, query_aug = sides[head]
            picked = query_aug[start:stop]
            diag = jnp.where(allowed, dot_nt(key_aug[start:stop], picked), NEG)
            top = jnp.max(diag, axis=0, keepdims=True)
            if start:
                early = dot_nt(key_aug[:start], picked)
                top = jnp.maximum(top, jnp.max(early, axis=0, keepdims=True))
            diag = jnp.exp(diag - top)
            total = jnp.sum(diag, axis=0, keepdims=True)
            value_rows = values_t[head * HEAD : (head + 1) * HEAD]
            out = dot_nn(value_rows[:, start:stop], diag.astype(BF16))
            if start:
                early = jnp.exp(early - top)
                total = total + jnp.sum(early, axis=0, keepdims=True)
                out = out + dot_nn(value_rows[:, :start], early.astype(BF16))
            outs.append(out / total)
            shift_ref[pl.ds(group * per_group + head, 1), start:stop] = -(top + jnp.log(total))
        block = jnp.transpose(jnp.concatenate(outs, axis=0))
        att_ref[start:stop] = block.astype(BF16)
        gated_ref[start:stop] = (block * jax.nn.sigmoid(gate_ref[start:stop])).astype(BF16)


def attend_back_body(
    q_ref, k_ref, v_ref, gate_ref, att_ref, grad_ref, logit_ref, bias_ref, shift_ref, keyb_ref,
    out_ref, bias_out_ref, low_ref, dk_ref, dv_ref, row_ref, col_ref,
    *, per_group, groups,
):
    group = pl.program_id(1)
    wide = per_group * HEAD
    part = groups * wide

    def columns(which):
        first = which * part + (PAD if which == 3 else 0)
        if groups == 1:
            return slice(first, first + wide)
        return pl.ds(pl.multiple_of(first + group * wide, wide), wide)

    @pl.when(group == 0)
    def _():
        row_ref[...] = jnp.zeros(row_ref.shape, F32)
        col_ref[...] = jnp.zeros(col_ref.shape, F32)

    lane = lax.broadcasted_iota(jnp.int32, (SLOTS, wide), 1)
    lane_all = lax.broadcasted_iota(jnp.int32, (SLOTS, PAD), 1)
    sig = jax.nn.sigmoid(gate_ref[...])
    grad_gated = grad_ref[...].astype(F32)
    grad_att = grad_gated * sig
    out_ref[:, columns(3)] = (grad_att * att_ref[...].astype(F32) * (1.0 - sig)).astype(BF16)
    low_ref[...] = grad_att.astype(BF16)
    queries = q_ref[...].astype(F32)
    keys = k_ref[...].astype(F32)
    keys_t = jnp.transpose(keys).astype(BF16)
    ones = jnp.ones((16, SLOTS), BF16)
    allowed = causal(BLOCK)
    grad_low = low_ref[...].astype(F32)
    sides = []
    for head in range(per_group):
        spare = HEAD if head == 0 else 0
        bias = pick_lane(keyb_ref[...], lane_all, group * per_group + head)
        sides.append(
            (
                key_side(keys, bias, lane, head, spare),
                query_side(queries, lane, head, spare),
                jnp.where(head_span(lane, head), grad_low, 0.0).astype(BF16),
                jnp.concatenate([keys_t[head * HEAD : (head + 1) * HEAD], ones], axis=0),
            )
        )
    for start in reversed(range(0, SLOTS, BLOCK)):
        stop = start + BLOCK
        last = stop == SLOTS
        outs = []
        for head in range(per_group):
            key_aug, query_aug, grad_own, key_rows = sides[head]
            picked = query_aug[start:stop]
            grads = grad_own[start:stop]
            shift = shift_ref[pl.ds(group * per_group + head, 1), start:stop]
            spans = [(start, stop)] + ([(0, start)] if start else [])
            weights = []
            inner = jnp.zeros((1, BLOCK), F32)
            for low, high in spans:
                score = dot_nt(key_aug[low:high], picked) + shift
                if low == start:
                    score = jnp.where(allowed, score, NEG)
                soft = jnp.exp(score)
                grad_soft = dot_nt(v_ref[low:high], grads)
                inner = inner + jnp.sum(soft * grad_soft, axis=0, keepdims=True)
                weights.append((soft, grad_soft))
            out = jnp.zeros((HEAD + 16, BLOCK), F32)
            for (low, high), (soft, grad_soft) in zip(spans, weights):
                grad_score = (soft * (grad_soft - inner)).astype(BF16)
                key_part = dot_nn(grad_score, picked)
                value_part = dot_nn(soft.astype(BF16), grads)
                if last:
                    dk_ref[head, low:high] = key_part
                    if head == 0:
                        dv_ref[low:high] = value_part
                    else:
                        dv_ref[low:high] += value_part
                else:
                    dk_ref[head, low:high] += key_part
                    dv_ref[low:high] += value_part
                out = out + dot_nn(key_rows[:, low:high], grad_score)
            outs.append(out[:HEAD] * HEAD ** (-0.5))
            row_ref[pl.ds(group * per_group + head, 1), start:stop] = out[HEAD : HEAD + 1]
        out_ref[start:stop, columns(0)] = jnp.transpose(jnp.concatenate(outs, axis=0)).astype(BF16)
    grad_keys = dk_ref[0]
    for head in range(per_group):
        spare = HEAD if head == 0 else 0
        found = dk_ref[head]
        if head:
            grad_keys = jnp.where(head_span(lane, head), found, grad_keys)
        sums = pick_lane(found, lane, spare)
        col_ref[...] = jnp.where(lane_all == group * per_group + head, sums, col_ref[...])
    out_ref[:, columns(1)] = grad_keys.astype(BF16)
    out_ref[:, columns(2)] = dv_ref[...].astype(BF16)

    @pl.when(group == groups - 1)
    def _():
        grad_decay = jnp.transpose(row_ref[...]) - col_ref[...]
        logit = logit_ref[...] + bias_ref[0:1]
        grad_logit = running_sum(grad_decay, True) * jax.nn.sigmoid(-logit)
        out_ref[:, 3 * part : 3 * part + PAD] = grad_logit.astype(BF16)
        bias_out_ref[...] = jnp.broadcast_to(jnp.sum(grad_logit, axis=0, keepdims=True), (8, PAD))


def head_blocks(part):
    heads = part // HEAD
    per_group = 2 if heads % 2 == 0 else heads
    groups = heads // per_group
    wide = per_group * HEAD

    def of(array, which, count):
        if part % 128 == 0:
            return array, pl.BlockSpec((SLOTS, wide), lambda s, g: (s, which * groups + g))
        return (
            array[:, which * part : (which + 1) * part],
            pl.BlockSpec((SLOTS, wide), lambda s, g: (s, g)),
        )

    return per_group, groups, wide, of


def logit_block(gate_logit):
    return gate_logit, pl.BlockSpec((SLOTS, PAD), lambda s, g: (s, 0))


def gate_block(gate_logit, part, wide):
    if part % 128 == 0:
        return gate_logit, pl.BlockSpec((SLOTS, wide), lambda s, g: (s, g + PAD // wide))
    return gate_logit[:, PAD:], pl.BlockSpec((SLOTS, wide), lambda s, g: (s, g))


def attend(proj, gate_logit, bias_rows, lengths, part):
    rows = proj.shape[0]
    seqs = rows // SLOTS
    per_group, groups, wide, of = head_blocks(part)
    fix = lambda f: (lambda s, g, lengths: f(s, g))
    parts = [of(proj, 0, 3), of(proj, 1, 3), of(proj, 2, 3), gate_block(gate_logit, part, wide)]
    parts.append(logit_block(gate_logit))
    parts.append((bias_rows, pl.BlockSpec((8, PAD), lambda s, g: (0, 0))))
    wide_spec = pl.BlockSpec((SLOTS, wide), lambda s, g: (s, g))
    outs = [
        (jax.ShapeDtypeStruct((rows, part), BF16), wide_spec),
        (jax.ShapeDtypeStruct((rows, part), BF16), wide_spec),
        (jax.ShapeDtypeStruct((seqs * PAD, SLOTS), F32), pl.BlockSpec((PAD, SLOTS), lambda s, g: (s, 0))),
        (jax.ShapeDtypeStruct((rows, PAD), F32), pl.BlockSpec((SLOTS, PAD), lambda s, g: (s, 0))),
    ]
    respec = lambda spec: pl.BlockSpec(spec.block_shape, fix(spec.index_map))
    return pl.pallas_call(
        functools.partial(attend_body, per_group=per_group),
        out_shape=[shape for shape, _ in outs],
        grid_spec=pltpu.PrefetchScalarGridSpec(
            num_scalar_prefetch=1,
            grid=(seqs, groups),
            in_specs=[respec(spec) for _, spec in parts],
            out_specs=[respec(spec) for _, spec in outs],
        ),
        compiler_params=pltpu.CompilerParams(
            dimension_semantics=("arbitrary", "arbitrary"), vmem_limit_bytes=48 * 2**20
        ),
        name="attend",
    )(lengths, *[array for array, _ in parts])


def attend_back(proj, gate_logit, attended, grad_gated, bias_rows, shift, keyb, part):
    rows = proj.shape[0]
    seqs = rows // SLOTS
    per_group, groups, wide, of = head_blocks(part)
    parts = [of(proj, 0, 3), of(proj, 1, 3), of(proj, 2, 3), gate_block(gate_logit, part, wide)]
    parts += [of(attended, 0, 1), of(grad_gated, 0, 1)]
    parts.append(logit_block(gate_logit))
    parts.append((bias_rows, pl.BlockSpec((8, PAD), lambda s, g: (0, 0))))
    parts.append((shift, pl.BlockSpec((PAD, SLOTS), lambda s, g: (s, 0))))
    parts.append((keyb, pl.BlockSpec((SLOTS, PAD), lambda s, g: (s, 0))))
    total = 4 * part + PAD
    return pl.pallas_call(
        functools.partial(attend_back_body, per_group=per_group, groups=groups),
        out_shape=[
            jax.ShapeDtypeStruct((rows, total), BF16),
            jax.ShapeDtypeStruct((seqs * 8, PAD), F32),
        ],
        grid=(seqs, groups),
        in_specs=[spec for _, spec in parts],
        out_specs=[
            pl.BlockSpec((SLOTS, total), lambda s, g: (s, 0)),
            pl.BlockSpec((8, PAD), lambda s, g: (s, 0)),
        ],
        scratch_shapes=[
            pltpu.VMEM((SLOTS, wide), BF16),
            pltpu.VMEM((per_group, SLOTS, wide), F32),
            pltpu.VMEM((SLOTS, wide), F32),
            pltpu.VMEM((PAD, SLOTS), F32),
            pltpu.VMEM((SLOTS, PAD), F32),
        ],
        compiler_params=pltpu.CompilerParams(
            dimension_semantics=("arbitrary", "arbitrary"), vmem_limit_bytes=56 * 2**20
        ),
        name="attend_back",
    )(*[array for array, _ in parts])


def on_device(
    layer_input,
    gain_attn,
    w_attn,
    w_forget,
    forget_bias,
    w_out,
    gain_mlp,
    w_mlp,
    w_down,
    lengths,
    cotangent,
):
    own_rows, width = layer_input.shape
    group_seqs = lengths.shape[0]
    part = w_attn.shape[2]
    heads_dev = part // HEAD
    units = w_mlp.shape[2]
    own_d = w_attn.shape[0]
    tensor_index = lax.axis_index("tensor")
    bias_own = lax.dynamic_slice_in_dim(forget_bias, tensor_index * heads_dev, heads_dev)
    positions = tensor_index * own_rows + jnp.arange(own_rows, dtype=jnp.int32)
    seq_of_row = positions // SLOTS
    matches = seq_of_row[:, None] == jnp.arange(group_seqs, dtype=jnp.int32)[None, :]
    own_lengths = jnp.sum(jnp.where(matches, lengths[None, :], 0), axis=1)
    valid = (positions % SLOTS < own_lengths).astype(F32)[:, None]

    attn_shard = jnp.concatenate(
        [
            w_attn[:, :3].reshape(own_d, 3 * part),
            jnp.pad(w_forget, ((0, 0), (0, PAD - heads_dev))),
            w_attn[:, 3],
        ],
        axis=1,
    )
    attn_cols = 4 * part + PAD
    first_full = gather_dp(jnp.concatenate([attn_shard, w_out.T], axis=1))
    second_shard = jnp.concatenate([w_down.T, w_mlp.reshape(own_d, 2 * units)], axis=1)
    input_wide = layer_input.astype(F32)
    scaled_attn, inverse_attn = norm_parts(input_wide)
    normed_all = share_rows((scaled_attn * gain_attn).astype(BF16))
    grad_final = cotangent.astype(F32) * valid
    grad_final_all = share_rows(grad_final.astype(BF16))
    first_full, second_shard, normed_all, grad_final_all = hold(
        first_full, second_shard, normed_all, grad_final_all
    )
    second_full = gather_dp(second_shard)
    attn_full, out_full = (first_full[:, :attn_cols], first_full[:, attn_cols:])
    down_full, mlp_full = (second_full[:, :units], second_full[:, units:])

    proj = dot_nn(normed_all, attn_full[:, : 3 * part]).astype(BF16)
    gate_logit = dot_nn(normed_all, attn_full[:, 3 * part :])
    bias_rows = jnp.broadcast_to(jnp.pad(bias_own, (0, PAD - heads_dev))[None, :], (8, PAD))
    gated, attended, shift, keyb = attend(proj, gate_logit, bias_rows, lengths, part)

    def attn_term(first_row, row_count):
        return dot_nt(lax.dynamic_slice_in_dim(gated, first_row, row_count), out_full)

    leaving, staying = term_parts(attn_term, own_rows)
    arrived, staying = hold(cross(leaving), staying)
    middle = input_wide + (staying + arrived.astype(F32))
    scaled_mlp, inverse_mlp = norm_parts(middle)
    normed_mid = share_rows((scaled_mlp * gain_mlp).astype(BF16))
    grad_hidden = dot_nn(grad_final_all, down_full)
    normed_mid, grad_hidden = hold(normed_mid, grad_hidden)
    gate_pre = dot_nn(normed_mid, mlp_full[:, :units])
    up_pre = dot_nn(normed_mid, mlp_full[:, units:])
    gate_s = jax.nn.sigmoid(gate_pre)
    silu = gate_pre * gate_s
    hidden = (silu * up_pre).astype(BF16)
    grad_gate = (grad_hidden * up_pre * gate_s * (1.0 + gate_pre * (1.0 - gate_s))).astype(BF16)
    grad_up = (grad_hidden * silu).astype(BF16)
    grad_pair = jnp.concatenate([grad_gate, grad_up], axis=1)

    def mlp_back_term(first_row, row_count):
        return dot_nt(lax.dynamic_slice_in_dim(grad_pair, first_row, row_count), mlp_full)

    down_grad = dot_tn(grad_final_all, hidden).astype(BF16)
    down_part = scatter_dp(down_grad)
    leaving, staying = term_parts(mlp_back_term, own_rows)
    mlp_grad = dot_tn(normed_mid, grad_pair).astype(BF16)
    arrived, staying, mlp_grad = hold(cross(leaving), staying, mlp_grad)
    mlp_part = scatter_dp(mlp_grad)
    grad_normed_mlp = staying + arrived.astype(F32)

    gain_mlp_part = jnp.sum(scaled_mlp * grad_normed_mlp, axis=0)
    grad_middle = grad_final + norm_back(grad_normed_mlp, scaled_mlp, inverse_mlp, gain_mlp)
    grad_middle_low, hidden = hold(grad_middle.astype(BF16), hidden)

    def mlp_term(first_row, row_count):
        return dot_nt(lax.dynamic_slice_in_dim(hidden, first_row, row_count), down_full)

    leaving, staying = term_parts(mlp_term, own_rows)
    grad_branch_all, leaving, staying = hold(share_rows(grad_middle_low), leaving, staying)
    arrived_out = cross(leaving)

    grad_gated = dot_nn(grad_branch_all, out_full).astype(BF16)
    grad_proj, bias_sums = attend_back(
        proj, gate_logit, attended, grad_gated, bias_rows, shift, keyb, part
    )
    grad_proj, arrived_out = hold(grad_proj, arrived_out)
    layer_output = (valid * (middle + (staying + arrived_out.astype(F32)))).astype(BF16)
    bias_part = jnp.sum(bias_sums.reshape(group_seqs, 8, PAD)[:, 0, :heads_dev], axis=0)

    def attn_back_term(first_row, row_count):
        return dot_nt(lax.dynamic_slice_in_dim(grad_proj, first_row, row_count), attn_full)

    bias_full = lax.dynamic_update_slice_in_dim(
        jnp.zeros(forget_bias.shape, F32), bias_part, tensor_index * heads_dev, 0
    )
    heads = forget_bias.shape[0]

    def finish(arrived):
        grad_normed_attn = staying + arrived.astype(F32)
        grad_input = grad_middle + norm_back(grad_normed_attn, scaled_attn, inverse_attn, gain_attn)
        terms = [jnp.sum(scaled_attn * grad_normed_attn, axis=0), gain_mlp_part]
        terms.append(jnp.pad(bias_full, (0, -heads % 128)))
        return grad_input, jnp.concatenate(terms).reshape(-1, 128)

    leaving, staying = term_parts(attn_back_term, own_rows)
    leaving, grad_later = hold(leaving, grad_proj)
    arrived_back = cross(leaving)
    grad_a = dot_tn(normed_all, grad_later[:, : 2 * part]).astype(BF16)
    grad_b = dot_tn(normed_all, grad_later[:, 2 * part :]).astype(BF16)
    size = lax.axis_size("dp")
    tensor_size = lax.axis_size("tensor")
    if size % 4 or size & (size - 1) or tensor_size & (tensor_size - 1):
        part_a, part_b = (scatter_dp(grad_a).astype(F32), scatter_dp(grad_b).astype(F32))
        out_part = scatter_dp(dot_tn(grad_branch_all, gated).astype(BF16))
        grad_input, sums = finish(arrived_back)
        sums = lax.psum(sums, ("dp", "tensor"))
    else:
        half_a = over_core(grad_a)
        half_a, gated, grad_branch_all = hold(half_a, gated, grad_branch_all)
        side_a = side_pieces(half_a, 1)
        half_b = over_core(grad_b)
        out_grad = dot_tn(grad_branch_all, gated).astype(BF16)
        out_layers = layer_pieces(over_core(out_grad))
        side_a, half_b, out_layers, arrived_back = hold(side_a, half_b, out_layers, arrived_back)
        layers_a = layer_pieces(total(side_a).astype(BF16))
        side_b = side_pieces(half_b, 1)
        grad_input, sums = finish(arrived_back)
        sums = add_traded(sums, "dp", [1])
        sums = add_traded(sums, "tensor", masks_of(tensor_size))
        layers_a, side_b, sums = hold(layers_a, side_b, sums)
        sums = add_traded(sums, "dp", masks_of(size)[2:])
        half_b, sums = hold(total(side_b).astype(BF16), sums)
        part_b = total(layer_pieces(half_b))
        part_a = total(layers_a)
        out_part = total(side_pieces(total(out_layers).astype(BF16), 0))
        sums = add_traded(sums, "dp", [2])
    sums = sums.reshape(-1)
    return (
        layer_output,
        grad_input,
        sums[:width],
        jnp.concatenate([part_a, part_b[:, :part], part_b[:, part + PAD :]], axis=1).reshape(
            own_d, 4, part
        ),
        part_b[:, part : part + heads_dev],
        sums[2 * width : 2 * width + heads],
        out_part.astype(F32).T,
        sums[width : 2 * width],
        mlp_part.astype(F32).reshape(own_d, 2, units),
        down_part.astype(F32).T,
    )


def solution(mesh):
    placed = (
        P(("dp", "tensor"), None),
        P(),
        P("dp", None, "tensor"),
        P("dp", "tensor"),
        P(),
        P("tensor", "dp"),
        P(),
        P("dp", None, "tensor"),
        P("tensor", "dp"),
        P("dp"),
        P(("dp", "tensor"), None),
    )

    return jax.shard_map(
        on_device,
        mesh=mesh,
        in_specs=placed,
        out_specs=(
            P(("dp", "tensor"), None),
            P(("dp", "tensor"), None),
            P(),
            P("dp", None, "tensor"),
            P("dp", "tensor"),
            P(),
            P("tensor", "dp"),
            P(),
            P("dp", None, "tensor"),
            P("tensor", "dp"),
        ),
        check_vma=False,
    )
```

```python
import functools

import jax
import jax.numpy as jnp
from jax import lax
from jax.experimental import pallas as pl
from jax.experimental.pallas import tpu as pltpu
from jax.sharding import PartitionSpec as P

HEAD = 64
SLOTS = 1024
EPS = 1e-06
PAD = 128
BLOCK = 256
NEG = -1e30

BF16 = jnp.bfloat16
F32 = jnp.float32


def norm_parts(rows):
    inverse = lax.rsqrt(jnp.mean(rows * rows, axis=-1, keepdims=True) + EPS)
    return (rows * inverse, inverse)


def norm_back(grad_normed, scaled, inverse, gain):
    grad_scaled = grad_normed * gain
    inner_sum = jnp.mean(grad_scaled * scaled, axis=-1, keepdims=True)
    return inverse * (grad_scaled - scaled * inner_sum)


def dot_nn(a, b):
    return lax.dot_general(a, b, (((1,), (0,)), ((), ())), preferred_element_type=F32)


def dot_nt(a, b):
    return lax.dot_general(a, b, (((1,), (1,)), ((), ())), preferred_element_type=F32)


def dot_tn(a, b):
    return lax.dot_general(a, b, (((0,), (0,)), ((), ())), preferred_element_type=F32)


def swap(rows):
    return lax.ppermute(rows, "tensor", [(0, 1), (1, 0)])


def share_rows(own):
    if lax.axis_size("tensor") != 2:
        return lax.all_gather(own, "tensor", axis=0, tiled=True)
    other = swap(own)
    first = lax.axis_index("tensor") == 0
    return jnp.concatenate([jnp.where(first, own, other), jnp.where(first, other, own)], axis=0)


def hold(*values):
    return lax.optimization_barrier(values)


def term_parts(term_fn, own_rows):
    size = lax.axis_size("tensor")
    if size != 2:
        return (term_fn(jnp.int32(0), own_rows * size).astype(BF16), jnp.zeros((), F32))
    index = lax.axis_index("tensor")
    return (
        term_fn((1 - index) * own_rows, own_rows).astype(BF16),
        term_fn(index * own_rows, own_rows),
    )


def cross(leaving):
    if lax.axis_size("tensor") != 2:
        return lax.psum_scatter(leaving, "tensor", scatter_dimension=0, tiled=True)
    return swap(leaving)


def gather_dp(shard):
    return lax.all_gather(shard, "dp", axis=0, tiled=True)


def scatter_dp(grad):
    return lax.psum_scatter(grad, "dp", scatter_dimension=0, tiled=True)


def trade(value, axis, mask):
    size = lax.axis_size(axis)
    return lax.ppermute(value, axis, [(i, i ^ mask) for i in range(size)])


def take(array, axis, index):
    return lax.dynamic_index_in_dim(array, index, axis, keepdims=False)


def over_core(grad):
    size = lax.axis_size("dp")
    core = lax.axis_index("dp") % 2
    grad = grad.reshape(size // 4, 2, 2, grad.shape[0] // size, grad.shape[1])
    arrived = trade(take(grad, 2, 1 - core), "dp", 1)
    return (take(grad, 2, core).astype(F32) + arrived.astype(F32)).astype(BF16)


def side_pieces(grad, axis):
    side = lax.axis_index("dp") // 2 % 2
    return [take(grad, axis, side), trade(take(grad, axis, 1 - side), "dp", 2)]


def layer_pieces(grad):
    layer = lax.axis_index("dp") // 4
    sent = [trade(take(grad, 0, layer ^ k), "dp", 4 * k) for k in range(1, grad.shape[0])]
    return [take(grad, 0, layer), *sent]


def total(pieces):
    result = pieces[0].astype(F32)
    for piece in pieces[1:]:
        result = result + piece.astype(F32)
    return result


def add_traded(value, axis, masks):
    for mask in masks:
        value = value + trade(value, axis, mask)
    return value


def masks_of(size):
    return [1 << k for k in range(size.bit_length() - 1)]


def head_span(lane, head):
    return (lane >= head * HEAD) & (lane < (head + 1) * HEAD)


def key_side(keys, bias, lane, head, spare):
    high = bias.astype(BF16).astype(F32)
    rest = bias - high
    mid = rest.astype(BF16).astype(F32)
    extra = jnp.where(
        lane == spare,
        high,
        jnp.where(lane == spare + 1, mid, jnp.where(lane == spare + 2, rest - mid, 0.0)),
    )
    return jnp.where(head_span(lane, head), keys, extra).astype(BF16)


def query_side(queries, lane, head, spare):
    ones = jnp.where((lane >= spare) & (lane < spare + 3), 1.0, 0.0)
    return jnp.where(head_span(lane, head), queries * HEAD ** (-0.5), ones).astype(BF16)


def pick_lane(rows, lane, index):
    return jnp.sum(jnp.where(lane == index, rows, 0.0), axis=1, keepdims=True)


def running_sum(rows, reverse):
    step = 1
    while step < SLOTS:
        zeros = jnp.zeros((step, rows.shape[1]), F32)
        if reverse:
            moved = jnp.concatenate([rows[step:], zeros], axis=0)
        else:
            moved = jnp.concatenate([zeros, rows[:-step]], axis=0)
        rows = rows + moved
        step *= 2
    return rows


def causal(block):
    key = lax.broadcasted_iota(jnp.int32, (block, block), 0)
    query = lax.broadcasted_iota(jnp.int32, (block, block), 1)
    return key <= query


def attend_body(
    lengths, q_ref, k_ref, v_ref, gate_ref, logit_ref, bias_ref, gated_ref, att_ref, shift_ref, keyb_ref,
    *, per_group,
):
    seq = pl.program_id(0)
    group = pl.program_id(1)
    wide = per_group * HEAD

    @pl.when(group == 0)
    def _():
        logit = logit_ref[...] + bias_ref[0:1]
        forget = jnp.minimum(logit, 0.0) - jnp.log1p(jnp.exp(-jnp.abs(logit)))
        slot = lax.broadcasted_iota(jnp.int32, (SLOTS, PAD), 0)
        keyb_ref[...] = jnp.where(slot < lengths[seq], -running_sum(forget, False), NEG)

    lane = lax.broadcasted_iota(jnp.int32, (SLOTS, wide), 1)
    lane_all = lax.broadcasted_iota(jnp.int32, (SLOTS, PAD), 1)
    queries = q_ref[...].astype(F32)
    keys = k_ref[...].astype(F32)
    values_t = jnp.transpose(v_ref[...].astype(F32)).astype(BF16)
    allowed = causal(BLOCK)
    sides = []
    for head in range(per_group):
        spare = HEAD if head == 0 else 0
        bias = pick_lane(keyb_ref[...], lane_all, group * per_group + head)
        sides.append(
            (key_side(keys, bias, lane, head, spare), query_side(queries, lane, head, spare))
        )
    for start in range(0, SLOTS, BLOCK):
        stop = start + BLOCK
        outs = []
        for head in range(per_group):
            key_aug, query_aug = sides[head]
            picked = query_aug[start:stop]
            diag = jnp.where(allowed, dot_nt(key_aug[start:stop], picked), NEG)
            top = jnp.max(diag, axis=0, keepdims=True)
            if start:
                early = dot_nt(key_aug[:start], picked)
                top = jnp.maximum(top, jnp.max(early, axis=0, keepdims=True))
            diag = jnp.exp(diag - top)
            total = jnp.sum(diag, axis=0, keepdims=True)
            value_rows = values_t[head * HEAD : (head + 1) * HEAD]
            out = dot_nn(value_rows[:, start:stop], diag.astype(BF16))
            if start:
                early = jnp.exp(early - top)
                total = total + jnp.sum(early, axis=0, keepdims=True)
                out = out + dot_nn(value_rows[:, :start], early.astype(BF16))
            outs.append(out / total)
            shift_ref[pl.ds(group * per_group + head, 1), start:stop] = -(top + jnp.log(total))
        block = jnp.transpose(jnp.concatenate(outs, axis=0))
        att_ref[start:stop] = block.astype(BF16)
        gated_ref[start:stop] = (block * jax.nn.sigmoid(gate_ref[start:stop])).astype(BF16)


def attend_back_body(
    q_ref, k_ref, v_ref, gate_ref, att_ref, grad_ref, logit_ref, bias_ref, shift_ref, keyb_ref,
    out_ref, bias_out_ref, low_ref, dk_ref, dv_ref, row_ref, col_ref,
    *, per_group, groups,
):
    group = pl.program_id(1)
    wide = per_group * HEAD
    part = groups * wide

    def columns(which):
        first = which * part + (PAD if which == 3 else 0)
        if groups == 1:
            return slice(first, first + wide)
        return pl.ds(pl.multiple_of(first + group * wide, wide), wide)

    @pl.when(group == 0)
    def _():
        row_ref[...] = jnp.zeros(row_ref.shape, F32)
        col_ref[...] = jnp.zeros(col_ref.shape, F32)

    lane = lax.broadcasted_iota(jnp.int32, (SLOTS, wide), 1)
    lane_all = lax.broadcasted_iota(jnp.int32, (SLOTS, PAD), 1)
    sig = jax.nn.sigmoid(gate_ref[...])
    grad_gated = grad_ref[...].astype(F32)
    grad_att = grad_gated * sig
    out_ref[:, columns(3)] = (grad_att * att_ref[...].astype(F32) * (1.0 - sig)).astype(BF16)
    low_ref[...] = grad_att.astype(BF16)
    queries = q_ref[...].astype(F32)
    keys = k_ref[...].astype(F32)
    keys_t = jnp.transpose(keys).astype(BF16)
    ones = jnp.ones((16, SLOTS), BF16)
    allowed = causal(BLOCK)
    grad_low = low_ref[...].astype(F32)
    sides = []
    for head in range(per_group):
        spare = HEAD if head == 0 else 0
        bias = pick_lane(keyb_ref[...], lane_all, group * per_group + head)
        sides.append(
            (
                key_side(keys, bias, lane, head, spare),
                query_side(queries, lane, head, spare),
                jnp.where(head_span(lane, head), grad_low, 0.0).astype(BF16),
                jnp.concatenate([keys_t[head * HEAD : (head + 1) * HEAD], ones], axis=0),
            )
        )
    for start in reversed(range(0, SLOTS, BLOCK)):
        stop = start + BLOCK
        last = stop == SLOTS
        outs = []
        for head in range(per_group):
            key_aug, query_aug, grad_own, key_rows = sides[head]
            picked = query_aug[start:stop]
            grads = grad_own[start:stop]
            shift = shift_ref[pl.ds(group * per_group + head, 1), start:stop]
            spans = [(start, stop)] + ([(0, start)] if start else [])
            weights = []
            inner = jnp.zeros((1, BLOCK), F32)
            for low, high in spans:
                score = dot_nt(key_aug[low:high], picked) + shift
                if low == start:
                    score = jnp.where(allowed, score, NEG)
                soft = jnp.exp(score)
                grad_soft = dot_nt(v_ref[low:high], grads)
                inner = inner + jnp.sum(soft * grad_soft, axis=0, keepdims=True)
                weights.append((soft, grad_soft))
            out = jnp.zeros((HEAD + 16, BLOCK), F32)
            for (low, high), (soft, grad_soft) in zip(spans, weights):
                grad_score = (soft * (grad_soft - inner)).astype(BF16)
                key_part = dot_nn(grad_score, picked)
                value_part = dot_nn(soft.astype(BF16), grads)
                if last:
                    dk_ref[head, low:high] = key_part
                    if head == 0:
                        dv_ref[low:high] = value_part
                    else:
                        dv_ref[low:high] += value_part
                else:
                    dk_ref[head, low:high] += key_part
                    dv_ref[low:high] += value_part
                out = out + dot_nn(key_rows[:, low:high], grad_score)
            outs.append(out[:HEAD] * HEAD ** (-0.5))
            row_ref[pl.ds(group * per_group + head, 1), start:stop] = out[HEAD : HEAD + 1]
        out_ref[start:stop, columns(0)] = jnp.transpose(jnp.concatenate(outs, axis=0)).astype(BF16)
    grad_keys = dk_ref[0]
    for head in range(per_group):
        spare = HEAD if head == 0 else 0
        found = dk_ref[head]
        if head:
            grad_keys = jnp.where(head_span(lane, head), found, grad_keys)
        sums = pick_lane(found, lane, spare)
        col_ref[...] = jnp.where(lane_all == group * per_group + head, sums, col_ref[...])
    out_ref[:, columns(1)] = grad_keys.astype(BF16)
    out_ref[:, columns(2)] = dv_ref[...].astype(BF16)

    @pl.when(group == groups - 1)
    def _():
        grad_decay = jnp.transpose(row_ref[...]) - col_ref[...]
        logit = logit_ref[...] + bias_ref[0:1]
        grad_logit = running_sum(grad_decay, True) * jax.nn.sigmoid(-logit)
        out_ref[:, 3 * part : 3 * part + PAD] = grad_logit.astype(BF16)
        bias_out_ref[...] = jnp.broadcast_to(jnp.sum(grad_logit, axis=0, keepdims=True), (8, PAD))


def head_blocks(part):
    heads = part // HEAD
    per_group = 2 if heads % 2 == 0 else heads
    groups = heads // per_group
    wide = per_group * HEAD

    def of(array, which, count):
        if part % 128 == 0:
            return array, pl.BlockSpec((SLOTS, wide), lambda s, g: (s, which * groups + g))
        return (
            array[:, which * part : (which + 1) * part],
            pl.BlockSpec((SLOTS, wide), lambda s, g: (s, g)),
        )

    return per_group, groups, wide, of


def logit_block(gate_logit):
    return gate_logit, pl.BlockSpec((SLOTS, PAD), lambda s, g: (s, 0))


def gate_block(gate_logit, part, wide):
    if part % 128 == 0:
        return gate_logit, pl.BlockSpec((SLOTS, wide), lambda s, g: (s, g + PAD // wide))
    return gate_logit[:, PAD:], pl.BlockSpec((SLOTS, wide), lambda s, g: (s, g))


def attend(proj, gate_logit, bias_rows, lengths, part):
    rows = proj.shape[0]
    seqs = rows // SLOTS
    per_group, groups, wide, of = head_blocks(part)
    fix = lambda f: (lambda s, g, lengths: f(s, g))
    parts = [of(proj, 0, 3), of(proj, 1, 3), of(proj, 2, 3), gate_block(gate_logit, part, wide)]
    parts.append(logit_block(gate_logit))
    parts.append((bias_rows, pl.BlockSpec((8, PAD), lambda s, g: (0, 0))))
    wide_spec = pl.BlockSpec((SLOTS, wide), lambda s, g: (s, g))
    outs = [
        (jax.ShapeDtypeStruct((rows, part), BF16), wide_spec),
        (jax.ShapeDtypeStruct((rows, part), BF16), wide_spec),
        (jax.ShapeDtypeStruct((seqs * PAD, SLOTS), F32), pl.BlockSpec((PAD, SLOTS), lambda s, g: (s, 0))),
        (jax.ShapeDtypeStruct((rows, PAD), F32), pl.BlockSpec((SLOTS, PAD), lambda s, g: (s, 0))),
    ]
    respec = lambda spec: pl.BlockSpec(spec.block_shape, fix(spec.index_map))
    return pl.pallas_call(
        functools.partial(attend_body, per_group=per_group),
        out_shape=[shape for shape, _ in outs],
        grid_spec=pltpu.PrefetchScalarGridSpec(
            num_scalar_prefetch=1,
            grid=(seqs, groups),
            in_specs=[respec(spec) for _, spec in parts],
            out_specs=[respec(spec) for _, spec in outs],
        ),
        compiler_params=pltpu.CompilerParams(
            dimension_semantics=("arbitrary", "arbitrary"), vmem_limit_bytes=48 * 2**20
        ),
        name="attend",
    )(lengths, *[array for array, _ in parts])


def attend_back(proj, gate_logit, attended, grad_gated, bias_rows, shift, keyb, part):
    rows = proj.shape[0]
    seqs = rows // SLOTS
    per_group, groups, wide, of = head_blocks(part)
    parts = [of(proj, 0, 3), of(proj, 1, 3), of(proj, 2, 3), gate_block(gate_logit, part, wide)]
    parts += [of(attended, 0, 1), of(grad_gated, 0, 1)]
    parts.append(logit_block(gate_logit))
    parts.append((bias_rows, pl.BlockSpec((8, PAD), lambda s, g: (0, 0))))
    parts.append((shift, pl.BlockSpec((PAD, SLOTS), lambda s, g: (s, 0))))
    parts.append((keyb, pl.BlockSpec((SLOTS, PAD), lambda s, g: (s, 0))))
    total = 4 * part + PAD
    return pl.pallas_call(
        functools.partial(attend_back_body, per_group=per_group, groups=groups),
        out_shape=[
            jax.ShapeDtypeStruct((rows, total), BF16),
            jax.ShapeDtypeStruct((seqs * 8, PAD), F32),
        ],
        grid=(seqs, groups),
        in_specs=[spec for _, spec in parts],
        out_specs=[
            pl.BlockSpec((SLOTS, total), lambda s, g: (s, 0)),
            pl.BlockSpec((8, PAD), lambda s, g: (s, 0)),
        ],
        scratch_shapes=[
            pltpu.VMEM((SLOTS, wide), BF16),
            pltpu.VMEM((per_group, SLOTS, wide), F32),
            pltpu.VMEM((SLOTS, wide), F32),
            pltpu.VMEM((PAD, SLOTS), F32),
            pltpu.VMEM((SLOTS, PAD), F32),
        ],
        compiler_params=pltpu.CompilerParams(
            dimension_semantics=("arbitrary", "arbitrary"), vmem_limit_bytes=56 * 2**20
        ),
        name="attend_back",
    )(*[array for array, _ in parts])


def on_device(
    layer_input,
    gain_attn,
    w_attn,
    w_forget,
    forget_bias,
    w_out,
    gain_mlp,
    w_mlp,
    w_down,
    lengths,
    cotangent,
):
    own_rows, width = layer_input.shape
    group_seqs = lengths.shape[0]
    part = w_attn.shape[2]
    heads_dev = part // HEAD
    units = w_mlp.shape[2]
    own_d = w_attn.shape[0]
    tensor_index = lax.axis_index("tensor")
    bias_own = lax.dynamic_slice_in_dim(forget_bias, tensor_index * heads_dev, heads_dev)
    positions = tensor_index * own_rows + jnp.arange(own_rows, dtype=jnp.int32)
    seq_of_row = positions // SLOTS
    matches = seq_of_row[:, None] == jnp.arange(group_seqs, dtype=jnp.int32)[None, :]
    own_lengths = jnp.sum(jnp.where(matches, lengths[None, :], 0), axis=1)
    valid = (positions % SLOTS < own_lengths).astype(F32)[:, None]

    attn_shard = jnp.concatenate(
        [
            w_attn[:, :3].reshape(own_d, 3 * part),
            jnp.pad(w_forget, ((0, 0), (0, PAD - heads_dev))),
            w_attn[:, 3],
        ],
        axis=1,
    )
    attn_cols = 4 * part + PAD
    first_full = gather_dp(jnp.concatenate([attn_shard, w_out.T], axis=1))
    second_shard = jnp.concatenate([w_down.T, w_mlp.reshape(own_d, 2 * units)], axis=1)
    input_wide = layer_input.astype(F32)
    scaled_attn, inverse_attn = norm_parts(input_wide)
    normed_all = share_rows((scaled_attn * gain_attn).astype(BF16))
    grad_final = cotangent.astype(F32) * valid
    grad_final_all = share_rows(grad_final.astype(BF16))
    first_full, second_shard, normed_all, grad_final_all = hold(
        first_full, second_shard, normed_all, grad_final_all
    )
    second_full = gather_dp(second_shard)
    attn_full, out_full = (first_full[:, :attn_cols], first_full[:, attn_cols:])
    down_full, mlp_full = (second_full[:, :units], second_full[:, units:])

    proj = dot_nn(normed_all, attn_full[:, : 3 * part]).astype(BF16)
    gate_logit = dot_nn(normed_all, attn_full[:, 3 * part :])
    bias_rows = jnp.broadcast_to(jnp.pad(bias_own, (0, PAD - heads_dev))[None, :], (8, PAD))
    gated, attended, shift, keyb = attend(proj, gate_logit, bias_rows, lengths, part)

    def attn_term(first_row, row_count):
        return dot_nt(lax.dynamic_slice_in_dim(gated, first_row, row_count), out_full)

    leaving, staying = term_parts(attn_term, own_rows)
    arrived, staying = hold(cross(leaving), staying)
    middle = input_wide + (staying + arrived.astype(F32))
    scaled_mlp, inverse_mlp = norm_parts(middle)
    normed_mid = share_rows((scaled_mlp * gain_mlp).astype(BF16))
    grad_hidden = dot_nn(grad_final_all, down_full)
    normed_mid, grad_hidden = hold(normed_mid, grad_hidden)
    gate_pre = dot_nn(normed_mid, mlp_full[:, :units])
    up_pre = dot_nn(normed_mid, mlp_full[:, units:])
    gate_s = jax.nn.sigmoid(gate_pre)
    silu = gate_pre * gate_s
    hidden = (silu * up_pre).astype(BF16)
    grad_gate = (grad_hidden * up_pre * gate_s * (1.0 + gate_pre * (1.0 - gate_s))).astype(BF16)
    grad_up = (grad_hidden * silu).astype(BF16)
    grad_pair = jnp.concatenate([grad_gate, grad_up], axis=1)

    def mlp_back_term(first_row, row_count):
        return dot_nt(lax.dynamic_slice_in_dim(grad_pair, first_row, row_count), mlp_full)

    down_grad = dot_tn(grad_final_all, hidden).astype(BF16)
    down_part = scatter_dp(down_grad)
    leaving, staying = term_parts(mlp_back_term, own_rows)
    mlp_grad = dot_tn(normed_mid, grad_pair).astype(BF16)
    arrived, staying, mlp_grad = hold(cross(leaving), staying, mlp_grad)
    mlp_part = scatter_dp(mlp_grad)
    grad_normed_mlp = staying + arrived.astype(F32)

    gain_mlp_part = jnp.sum(scaled_mlp * grad_normed_mlp, axis=0)
    grad_middle = grad_final + norm_back(grad_normed_mlp, scaled_mlp, inverse_mlp, gain_mlp)
    grad_middle_low, hidden = hold(grad_middle.astype(BF16), hidden)

    def mlp_term(first_row, row_count):
        return dot_nt(lax.dynamic_slice_in_dim(hidden, first_row, row_count), down_full)

    leaving, staying = term_parts(mlp_term, own_rows)
    grad_branch_all, leaving, staying = hold(share_rows(grad_middle_low), leaving, staying)
    arrived_out = cross(leaving)

    grad_gated = dot_nn(grad_branch_all, out_full).astype(BF16)
    grad_proj, bias_sums = attend_back(
        proj, gate_logit, attended, grad_gated, bias_rows, shift, keyb, part
    )
    grad_proj, arrived_out = hold(grad_proj, arrived_out)
    layer_output = (valid * (middle + (staying + arrived_out.astype(F32)))).astype(BF16)
    bias_part = jnp.sum(bias_sums.reshape(group_seqs, 8, PAD)[:, 0, :heads_dev], axis=0)

    def attn_back_term(first_row, row_count):
        return dot_nt(lax.dynamic_slice_in_dim(grad_proj, first_row, row_count), attn_full)

    bias_full = lax.dynamic_update_slice_in_dim(
        jnp.zeros(forget_bias.shape, F32), bias_part, tensor_index * heads_dev, 0
    )
    heads = forget_bias.shape[0]

    def finish(arrived):
        grad_normed_attn = staying + arrived.astype(F32)
        grad_input = grad_middle + norm_back(grad_normed_attn, scaled_attn, inverse_attn, gain_attn)
        terms = [jnp.sum(scaled_attn * grad_normed_attn, axis=0), gain_mlp_part]
        terms.append(jnp.pad(bias_full, (0, -heads % 128)))
        return grad_input, jnp.concatenate(terms).reshape(-1, 128)

    leaving, staying = term_parts(attn_back_term, own_rows)
    leaving, grad_later = hold(leaving, grad_proj)
    arrived_back = cross(leaving)
    grad_a = dot_tn(normed_all, grad_later[:, : 2 * part]).astype(BF16)
    grad_b = dot_tn(normed_all, grad_later[:, 2 * part :]).astype(BF16)
    size = lax.axis_size("dp")
    tensor_size = lax.axis_size("tensor")
    if size % 4 or size & (size - 1) or tensor_size & (tensor_size - 1):
        part_a, part_b = (scatter_dp(grad_a).astype(F32), scatter_dp(grad_b).astype(F32))
        out_part = scatter_dp(dot_tn(grad_branch_all, gated).astype(BF16))
        grad_input, sums = finish(arrived_back)
        sums = lax.psum(sums, ("dp", "tensor"))
    else:
        half_a = over_core(grad_a)
        half_a, gated, grad_branch_all = hold(half_a, gated, grad_branch_all)
        side_a = side_pieces(half_a, 1)
        half_b = over_core(grad_b)
        out_grad = dot_tn(grad_branch_all, gated).astype(BF16)
        out_half = over_core(out_grad)
        out_layers = layer_pieces(out_half)
        side_a, half_b, arrived_back, layer_output = hold(
            side_a, half_b, arrived_back, layer_output
        )
        layers_a = layer_pieces(total(side_a).astype(BF16))
        side_b = side_pieces(half_b, 1)
        grad_input, sums = finish(arrived_back)
        sums = add_traded(sums, "dp", [1])
        sums = add_traded(sums, "tensor", masks_of(tensor_size))
        sums = add_traded(sums, "dp", masks_of(size)[2:-1])
        layers_a, side_b, out_layers, sums = hold(layers_a, side_b, out_layers, sums)
        sums = add_traded(sums, "dp", masks_of(size)[2:][-1:])
        half_b, sums = hold(total(side_b).astype(BF16), sums)
        part_b = total(layer_pieces(half_b))
        part_a = total(layers_a)
        out_part = total(side_pieces(total(out_layers).astype(BF16), 0))
        sums = add_traded(sums, "dp", [2])
    sums = sums.reshape(-1)
    return (
        layer_output,
        grad_input,
        sums[:width],
        jnp.concatenate([part_a, part_b[:, :part], part_b[:, part + PAD :]], axis=1).reshape(
            own_d, 4, part
        ),
        part_b[:, part : part + heads_dev],
        sums[2 * width : 2 * width + heads],
        out_part.astype(F32).T,
        sums[width : 2 * width],
        mlp_part.astype(F32).reshape(own_d, 2, units),
        down_part.astype(F32).T,
    )


def solution(mesh):
    placed = (
        P(("dp", "tensor"), None),
        P(),
        P("dp", None, "tensor"),
        P("dp", "tensor"),
        P(),
        P("tensor", "dp"),
        P(),
        P("dp", None, "tensor"),
        P("tensor", "dp"),
        P("dp"),
        P(("dp", "tensor"), None),
    )

    return jax.shard_map(
        on_device,
        mesh=mesh,
        in_specs=placed,
        out_specs=(
            P(("dp", "tensor"), None),
            P(("dp", "tensor"), None),
            P(),
            P("dp", None, "tensor"),
            P("dp", "tensor"),
            P(),
            P("tensor", "dp"),
            P(),
            P("dp", None, "tensor"),
            P("tensor", "dp"),
        ),
        check_vma=False,
    )
```
